128 devices in a mesh: row: 4 (over y_lo, core), col: 32 (over y_hi, z, x).
Axes of the slice: x: 4, y: 4 (y_hi: 2, y_lo: 2; y = y_hi * 2 + y_lo), z: 4, core: 2. Of those that a mesh axis runs over, the one named last changes fastest.
Arguments:
- sky: bfloat16 [128, 1024, 4096], P(None, 'row', 'col'), may hold values from -80 to 80
- kernel_widths: int32 [2], replicated, may hold values from 16 to 32, as said below
- prior_var: float32 [2, 128], replicated, may hold values from 0.05 to 0.5
- tile_region: int32 [4, 32], P('row', 'col'), may hold values from 0 to 7, as said below
- region_rank: int32 [8], replicated, may hold values from 2 to 8
Outputs:
- cleaned: bfloat16 [128, 1024, 4096], P(None, 'row', 'col')
The draws below stay inside these ranges and needn't reach their ends.
Inputs may be any that keep to these rules, and one draw needn't show every extreme that they name: `kernel_widths`: entry 0 is the half-width along the sky's rows (second dimension of sky), entry 1 along its columns; one of the two equals 32, the other is below 32. `tile_region`: each region holds exactly 16 tiles, anywhere on the sky.
All inputs are finite; a program needn't handle non-finite values.
Results may differ from the reference program's by a relative error of at most 0.0085.
Values may be sent and summed in bfloat16 or wider, within the bound.
A program may use at most 128 MiB of HBM per device.

```python
import functools
import math
import jax
import jax.numpy as jnp
from jax import lax

C = 128
TY = 256
TX = 128
HW = 32
MMAX = 8
TPR = 16
NY = 1024
NX = 4096
NREG = 8
N_ROW = 4
N_COL = 32


def draw_sky(key, part):
    keys = jax.random.split(key, 6)
    tiles_down = NY // TY
    tiles_across = NX // TX
    position = (2.0 * jnp.arange(C, dtype=jnp.float32) + 1.0) / C - 1.0
    scale = jnp.exp(jax.random.uniform(keys[0], (C, 1, 1), minval=math.log(0.3), maxval=math.log(3.0)))
    noise = jnp.clip(jax.random.normal(keys[1], (C, NY, NX)), -5.0, 5.0)
    amplitude = 0.4
    down = jnp.arange(NY, dtype=jnp.float32) / NY
    across = jnp.arange(NX, dtype=jnp.float32) / NX
    envelope = (1.0 + down)[:, None] * (1.0 + 2.0 * across)[None, :]
    tile_coef = jnp.clip(jax.random.normal(keys[2], (tiles_down, tiles_across, 6)), -3.0, 3.0)
    expanded = jnp.repeat(jnp.repeat(tile_coef, TY, axis=0), TX, axis=1)
    freq_down = jax.random.uniform(keys[3], (5, 3), minval=0.5, maxval=1.0 * tiles_down)
    freq_across = jax.random.uniform(keys[4], (5, 3), minval=0.5, maxval=0.5 * tiles_across)
    phases = jax.random.uniform(keys[5], (5, 3), minval=0.0, maxval=2.0 * math.pi)
    spectra = [jnp.ones_like(position), position]
    for order in range(2, 5):
        spectra.append(2.0 * position * spectra[-1] - spectra[-2])
    total = noise * scale
    first_field = None
    for order in range(5):
        field = jnp.zeros((NY, NX), jnp.float32)
        for wave in range(3):
            field = field + jnp.cos(2.0 * math.pi * (freq_down[order, wave] * down[:, None] + freq_across[order, wave] * across[None, :]) + phases[order, wave]) / 3.0
        if order == 0:
            first_field = field
        total = total + amplitude * spectra[order][:, None, None] * (envelope * expanded[:, :, order] * field)[None]
    bend = jnp.sin(3.0 * position[:, None, None] * (1.0 + 0.5 * expanded[None, :, :, 5]))
    total = total + 0.5 * bend * (envelope * first_field)[None]
    return total.astype(jnp.bfloat16)


def draw_kernel_widths(key, part):
    first, second = jax.random.split(key, 2)
    others = jax.random.randint(first, (2,), HW // 2, HW)
    picked = jax.random.randint(second, (), 0, 2)
    return jnp.where(jnp.arange(2) == picked, HW, others).astype(jnp.int32)


def draw_tile_region(key, part):
    tiles_down = NY // TY
    tiles_across = NX // TX
    shuffled = jax.random.permutation(key, tiles_down * tiles_across)
    return (shuffled // TPR).reshape(tiles_down, tiles_across).astype(jnp.int32)


def draw_region_rank(key, part):
    first, second = jax.random.split(key, 2)
    ranks = jax.random.randint(first, (NREG,), 2, MMAX + 1)
    shuffled = jax.random.permutation(second, NREG)
    ranks = ranks.at[shuffled[0]].set(MMAX)
    ranks = ranks.at[shuffled[1]].set(2)
    return ranks.astype(jnp.int32)


def setup_inputs(seed: int = 0) -> dict:
    key_of = jax.random.split(jax.random.key(seed), 6)
    return {
        "sky": draw_sky(jax.random.fold_in(key_of[5], 71), 0),
        "kernel_widths": draw_kernel_widths(jax.random.fold_in(key_of[5], 71), 0),
        "prior_var": jnp.clip(jnp.exp(jax.random.uniform(key_of[2], (2, C), jnp.float32, math.log(0.05), math.log(0.5))), 0.05, 0.5),
        "tile_region": draw_tile_region(jax.random.fold_in(key_of[5], 71), 0),
        "region_rank": draw_region_rank(jax.random.fold_in(key_of[5], 71), 0),
    }


def raised(offsets, half_width):
    spread = half_width.astype(jnp.float32)
    inside = jnp.abs(offsets) <= spread
    values = (1.0 + jnp.cos(math.pi * offsets / (spread + 1.0))) / (2.0 * spread + 2.0)
    return jnp.where(inside, values, jnp.zeros_like(values))

def chebyshev(chan_count, degree):
    position = (2.0 * jnp.arange(chan_count, dtype=jnp.float32) + 1.0) / chan_count - 1.0
    terms = [jnp.ones_like(position), position]
    for order in range(2, degree):
        terms.append(2.0 * position * terms[-1] - terms[-2])
    return jnp.stack(terms[:degree], axis=1)

def spd_solve(matrix, right_hand):
    factor = jnp.linalg.cholesky(matrix)
    middle = lax.linalg.triangular_solve(factor, right_hand, left_side=True, lower=True)
    return lax.linalg.triangular_solve(factor, middle, left_side=True, lower=True, transpose_a=True)

def projector(gram_sum, prior_row, keep_rank, pixels):
    chan_count = gram_sum.shape[0]
    cheb_basis = chebyshev(chan_count, MMAX)
    covariance = gram_sum / pixels + jnp.diag(prior_row)
    mixed = spd_solve(covariance, cheb_basis)
    keep_mask = (jnp.arange(MMAX) < keep_rank).astype(jnp.float32)
    kept_basis = cheb_basis * keep_mask
    kept_mixed = mixed * keep_mask
    small_matrix = jnp.dot(kept_basis.T, kept_mixed, precision=lax.Precision.HIGHEST) + jnp.diag(1.0 - keep_mask)
    weights = spd_solve(small_matrix, kept_mixed.T)
    return jnp.dot(kept_basis, weights, precision=lax.Precision.HIGHEST).astype(jnp.bfloat16)

def kernel_spectrum(length, half_width):
    total = length + 2 * HW
    index = jnp.arange(total, dtype=jnp.float32)
    offsets = jnp.where(index <= total / 2.0, index, index - total)
    taps = raised(offsets, half_width).astype(jnp.bfloat16).astype(jnp.float32)
    return jnp.fft.rfft(taps)

def along_axis(plane, spectrum, axis_number):
    length = plane.shape[axis_number]
    total = length + 2 * HW
    transformed = jnp.fft.rfft(plane, n=total, axis=axis_number)
    if axis_number == 0:
        shaped = spectrum[:, None]
    else:
        shaped = spectrum[None, :]
    result = jnp.fft.irfft(transformed * shaped, n=total, axis=axis_number)
    return lax.slice_in_dim(result, 0, length, axis=axis_number)

def reference(sky, kernel_widths, prior_var, tile_region, region_rank):
    chan_count = sky.shape[0]
    spectrum_y = kernel_spectrum(NY, kernel_widths[0])
    spectrum_x = kernel_spectrum(NX, kernel_widths[1])

    def filter_channel(plane):
        values = plane.astype(jnp.float32)
        smooth = along_axis(values, spectrum_y, 0).astype(jnp.bfloat16)
        coarse = along_axis(smooth.astype(jnp.float32), spectrum_x, 1).astype(jnp.bfloat16)
        fine = (values - coarse.astype(jnp.float32)).astype(jnp.bfloat16)
        return (coarse, fine)
    coarse, fine = lax.map(filter_channel, sky)
    row_ids = jnp.arange(N_ROW, dtype=jnp.int32)

    def slab_of(band, row_index):
        start = (row_index * TY).astype(jnp.int32)
        piece = lax.dynamic_slice_in_dim(band, start, TY, 1)
        return piece.astype(jnp.float32).reshape(chan_count, TY, N_COL, TX)

    def row_grams(row_index):
        grams = []
        for band in (coarse, fine):
            piece = slab_of(band, row_index)
            grams.append(jnp.einsum('cynx,dynx->ncd', piece, piece, precision=lax.Precision.HIGHEST))
        return jnp.stack(grams, axis=1)
    tile_grams = lax.map(row_grams, row_ids).reshape(N_ROW * N_COL, 2, chan_count, chan_count)
    region_ids = jnp.arange(NREG, dtype=jnp.int32)
    onehot = (tile_region.reshape(N_ROW * N_COL)[:, None] == region_ids[None, :]).astype(jnp.float32)
    region_gram = jnp.einsum('tr,tbcd->rbcd', onehot, tile_grams, precision=lax.Precision.HIGHEST)
    pixels = TPR * TY * TX
    single = functools.partial(projector, pixels=pixels)
    per_band = jax.vmap(single, in_axes=(0, 0, None))
    all_proj = jax.vmap(per_band, in_axes=(0, None, 0))(region_gram, prior_var, region_rank)
    tile_proj = all_proj[tile_region]

    def row_clean(row_index):
        proj_row = lax.dynamic_index_in_dim(tile_proj, row_index, 0, keepdims=False).astype(jnp.float32)
        coarse_piece = slab_of(coarse, row_index)
        fine_piece = slab_of(fine, row_index)
        removed = jnp.einsum('nij,jynx->iynx', proj_row[:, 0], coarse_piece, precision=lax.Precision.HIGHEST)
        removed = removed + jnp.einsum('nij,jynx->iynx', proj_row[:, 1], fine_piece, precision=lax.Precision.HIGHEST)
        result = coarse_piece + fine_piece - removed
        return result.astype(jnp.bfloat16).reshape(chan_count, TY, NX)
    blocks = lax.map(row_clean, row_ids)
    return jnp.transpose(blocks, (1, 0, 2, 3)).reshape(chan_count, NY, NX)
```

```python
import math
import functools
import jax
import jax.numpy as jnp
from jax import lax
from jax.experimental import pallas as pl
from jax.experimental.pallas import tpu as pltpu
from jax.sharding import PartitionSpec as P

HW = 32
MMAX = 8
TPR = 16
PLANE = 16
GROUP = 8
MESH = pl.DeviceIdType.MESH
HIGH = lax.Precision.HIGHEST


def gather_kernel(pk_ref, out_ref, first, slots, others, picked, last, s1, r1, s2, r2, s3, r3):
    row = lax.axis_index("row")
    col = lax.axis_index("col")
    part = lax.rem(col, PLANE)
    half = lax.div(col, PLANE)
    place = half * 4 + row

    def plane_peer(step):
        return (row, half * PLANE + lax.rem(part + step, PLANE))

    def group_peer(step):
        other = lax.rem(place + step, GROUP)
        return (lax.rem(other, 4), lax.div(other, 4) * PLANE + part)

    barrier = pltpu.get_barrier_semaphore()
    for step in range(1, PLANE):
        pl.semaphore_signal(barrier, inc=1, device_id=plane_peer(step), device_id_type=MESH)
    for step in range(1, GROUP):
        pl.semaphore_signal(barrier, inc=1, device_id=group_peer(step), device_id_type=MESH)
    pl.semaphore_wait(barrier, PLANE + GROUP - 2)

    one = []
    for step in range(1, PLANE):
        one.append(pltpu.make_async_remote_copy(
            src_ref=pk_ref.at[lax.rem(part + step, PLANE)], dst_ref=first.at[step],
            send_sem=s1.at[step], recv_sem=r1.at[step],
            device_id=plane_peer(step), device_id_type=MESH))
    for copy in one:
        copy.start()
    first[0] = pk_ref[part]
    for copy in one:
        copy.wait_recv()
    for region in range(8):
        total0 = jnp.zeros((8, 128), jnp.float32)
        total1 = jnp.zeros((8, 128), jnp.float32)
        for step in range(PLANE):
            flag = first[step, 2, region:region + 1, :]
            total0 = total0 + flag * first[step, 0]
            total1 = total1 + flag * first[step, 1]
        slots[region, 0] = total0
        slots[region, 1] = total1

    two = []
    for step in range(1, GROUP):
        two.append(pltpu.make_async_remote_copy(
            src_ref=slots, dst_ref=others.at[step],
            send_sem=s2.at[step], recv_sem=r2.at[step],
            device_id=group_peer(step), device_id_type=MESH))
    for copy in two:
        copy.start()
    for copy in two:
        copy.wait_recv()
    sums = []
    for region in range(8):
        pair = []
        for band in range(2):
            total = slots[region, band]
            for step in range(1, GROUP):
                total = total + others[step, region, band]
            pair.append(total)
        sums.append(pair)

    for step in range(PLANE):
        for band in range(2):
            total = jnp.zeros((8, 128), jnp.float32)
            for region in range(8):
                total = total + first[step, 2, region:region + 1, :] * sums[region][band]
            picked[step, band] = total
    three = []
    for step in range(1, PLANE):
        back = lax.rem(part + PLANE - step, PLANE)
        three.append(pltpu.make_async_remote_copy(
            src_ref=picked.at[step], dst_ref=last.at[part],
            send_sem=s3.at[step], recv_sem=r3.at[step],
            device_id=(row, half * PLANE + back), device_id_type=MESH))
    for copy in three:
        copy.start()
    last[part] = picked[0]
    for step in range(1, PLANE):
        ahead = lax.rem(part + step, PLANE)
        pltpu.make_async_remote_copy(
            src_ref=picked.at[step], dst_ref=last.at[ahead],
            send_sem=s3.at[step], recv_sem=r3.at[step],
            device_id=(row, half * PLANE + ahead), device_id_type=MESH).wait_recv()
    for index in range(PLANE):
        for band in range(2):
            out_ref[band, index * 8:index * 8 + 8, :] = last[index, band]
    for copy in one + two + three:
        copy.wait_send()


def region_grams(packed):
    return pl.pallas_call(
        gather_kernel,
        out_shape=jax.ShapeDtypeStruct((2, 128, 128), jnp.float32),
        in_specs=[pl.BlockSpec(memory_space=pltpu.VMEM)],
        out_specs=pl.BlockSpec(memory_space=pltpu.VMEM),
        scratch_shapes=[
            pltpu.VMEM((PLANE, 3, 8, 128), jnp.float32),
            pltpu.VMEM((8, 2, 8, 128), jnp.float32),
            pltpu.VMEM((GROUP, 8, 2, 8, 128), jnp.float32),
            pltpu.VMEM((PLANE, 2, 8, 128), jnp.float32),
            pltpu.VMEM((PLANE, 2, 8, 128), jnp.float32),
        ] + [pltpu.SemaphoreType.DMA((n,)) for n in (PLANE, PLANE, GROUP, GROUP, PLANE, PLANE)],
        compiler_params=pltpu.CompilerParams(collective_id=1, has_side_effects=True),
        name="region_sum",
    )(packed)


def weights_of(grams, priors, cheb_t, keep):
    lanes = lax.broadcasted_iota(jnp.int32, (8, 128), 1)
    subs = lax.broadcasted_iota(jnp.int32, (8, 128), 0)
    mats = []
    for band in range(2):
        blocks = []
        for i in range(16):
            block = grams[band][i * 8:i * 8 + 8, :]
            diag = jnp.where(lanes == subs + 8 * i, priors[band], 0.0)
            blocks.append(block / 524288.0 + diag)
        blocks.append(cheb_t)
        mats.append(blocks)
    for k in range(128):
        at, off = k // 8, k % 8
        hit = lanes[0:1, :] == k
        for band in range(2):
            m = mats[band]
            cols = [jnp.broadcast_to(b[:, k:k + 1], (8, 128)) for b in m]
            inv = 1.0 / cols[at][off:off + 1, :]
            line = m[at][off:off + 1, :] * inv
            line = jnp.where(hit, 1.0 - inv, line)
            mats[band] = [b - c * line for b, c in zip(m, cols)]
    out = []
    for band in range(2):
        mixed = mats[band][16] * keep
        kept = cheb_t * keep
        small = lax.dot_general(kept, mixed, (((1,), (1,)), ((), ())), precision=HIGH,
                                preferred_element_type=jnp.float32)
        eye = (lax.broadcasted_iota(jnp.int32, (8, 8), 0) == lax.broadcasted_iota(jnp.int32, (8, 8), 1))
        small = small + jnp.where(eye, 1.0 - keep[:, 0:8], 0.0)
        out.append((small, mixed))
    weights = []
    for small, mixed in out:
        for k in range(8):
            fac = small[:, k:k + 1]
            inv = 1.0 / fac[k:k + 1, :]
            shift = jnp.where(subs[:, 0:1] == k, 1.0, 0.0)
            fac = fac - shift
            srow = small[k:k + 1, :] * inv
            mrow = mixed[k:k + 1, :] * inv
            small = small - fac * srow
            mixed = mixed - fac * mrow
        weights.append(mixed)
    return weights


def solve_kernel(gram_ref, prior_ref, cheb_ref, keep_ref, out_ref):
    cheb_t = cheb_ref[...]
    keep = keep_ref[...]
    grams = [gram_ref[0], gram_ref[1]]
    priors = [prior_ref[0:1, :], prior_ref[1:2, :]]
    weights = weights_of(grams, priors, cheb_t, keep)
    kept = cheb_t * keep
    for band in range(2):
        proj = lax.dot_general(kept, weights[band], (((0,), (0,)), ((), ())), precision=HIGH,
                               preferred_element_type=jnp.float32)
        out_ref[band] = proj.astype(jnp.bfloat16)


def projectors(grams, prior_var, cheb_t, keep):
    return pl.pallas_call(
        solve_kernel,
        out_shape=jax.ShapeDtypeStruct((2, 128, 128), jnp.bfloat16),
        in_specs=[pl.BlockSpec(memory_space=pltpu.VMEM)] * 4,
        out_specs=pl.BlockSpec(memory_space=pltpu.VMEM),
        name="solve",
    )(grams, prior_var, cheb_t, keep)


def extended_2(cells, sides, width):
    for axis, dim in sides:
        count = lax.axis_size(axis)
        ends = count - 1
        head = lax.slice_in_dim(cells, 0, width, axis=dim)
        tail = lax.slice_in_dim(cells, cells.shape[dim] - width, cells.shape[dim], axis=dim)
        cells = jnp.concatenate(
            [
                lax.ppermute(tail, axis, [(i, (i + 1) % count) for i in range(ends)]),
                cells,
                lax.ppermute(head, axis, [((i + 1) % count, i) for i in range(ends)]),
            ],
            axis=dim,
        )
    return cells


def raised(offsets, half_width):
    spread = half_width.astype(jnp.float32)
    inside = jnp.abs(offsets) <= spread
    values = (1.0 + jnp.cos(math.pi * offsets / (spread + 1.0))) / (2.0 * spread + 2.0)
    return jnp.where(inside, values, jnp.zeros_like(values))


def toeplitz(length, half_width):
    inputs = jnp.arange(length + 2 * HW, dtype=jnp.float32)[:, None]
    outputs = jnp.arange(length, dtype=jnp.float32)[None, :]
    offsets = inputs - outputs - HW
    return raised(offsets, half_width).astype(jnp.bfloat16)


def chebyshev(chan_count, degree):
    position = (2.0 * jnp.arange(chan_count, dtype=jnp.float32) + 1.0) / chan_count - 1.0
    terms = [jnp.ones_like(position), position]
    for order in range(2, degree):
        terms.append(2.0 * position * terms[-1] - terms[-2])
    return jnp.stack(terms[:degree], axis=0)


def local(sky, kernel_widths, prior_var, tile_region, region_rank):
    chan_count, tile_rows, tile_cols = sky.shape
    down_table = toeplitz(tile_rows, kernel_widths[0])
    across_table = toeplitz(tile_cols, kernel_widths[1])
    extended = extended_2(sky, (("row", 1), ("col", 2)), HW)
    smooth = jnp.einsum(
        "cyx,yz->czx", extended, down_table, preferred_element_type=jnp.float32
    ).astype(jnp.bfloat16)
    coarse = jnp.einsum(
        "cyx,xz->cyz", smooth, across_table, preferred_element_type=jnp.float32
    ).astype(jnp.bfloat16)
    fine = (sky.astype(jnp.float32) - coarse.astype(jnp.float32)).astype(jnp.bfloat16)
    coarse_gram = jnp.einsum("cyx,dyx->cd", coarse, coarse, preferred_element_type=jnp.float32)
    fine_gram = jnp.einsum("cyx,dyx->cd", fine, fine, preferred_element_type=jnp.float32)
    region = tile_region[0, 0]
    flags = jnp.broadcast_to((jnp.arange(8) == region).astype(jnp.float32)[None, :, None], (PLANE, 8, 128))
    packed = jnp.stack(
        [coarse_gram.reshape(PLANE, 8, 128), fine_gram.reshape(PLANE, 8, 128), flags], axis=1)
    own_gram = region_grams(packed)
    keep_rank = lax.dynamic_index_in_dim(region_rank, region, 0, keepdims=False)
    keep = jnp.broadcast_to((jnp.arange(8) < keep_rank).astype(jnp.float32)[:, None], (8, 128))
    proj = projectors(own_gram, prior_var, chebyshev(chan_count, MMAX), keep)
    removed = jnp.einsum("ij,jyx->iyx", proj[0], coarse, preferred_element_type=jnp.float32)
    removed = removed + jnp.einsum("ij,jyx->iyx", proj[1], fine, preferred_element_type=jnp.float32)
    cleaned = coarse.astype(jnp.float32) + fine.astype(jnp.float32) - removed
    return cleaned.astype(jnp.bfloat16)


def solution(mesh):
    return jax.shard_map(
        local,
        mesh=mesh,
        in_specs=(P(None, "row", "col"), P(), P(), P("row", "col"), P()),
        out_specs=P(None, "row", "col"),
        check_vma=False,
    )
```

```python
import math
import jax
import jax.numpy as jnp
from jax import lax
from jax.experimental import pallas as pl
from jax.experimental.pallas import tpu as pltpu
from jax.sharding import PartitionSpec as P

HW = 32
MMAX = 8
TPR = 16
PLANE = 16
GROUP = 8
CHANS = 128
CHUNK = 64
ORDER = (1, 2, 0, 3)
MESH = pl.DeviceIdType.MESH
HIGH = lax.Precision.HIGHEST
NT = (((1,), (1,)), ((), ()))


def front_kernel(sky_ref, table_ref, flag_ref, bands_ref, gram_ref,
                 skyx, smooth, out_l, out_r, in_l, in_r, across, pick, flat_c, flat_f, stage, grams, pieces,
                 first, slots, others, picked, last,
                 sky_sem, ys, yr, xs, xr, stage_sem, s1, r1, s2, r2, s3, r3):
    row = lax.axis_index("row")
    col = lax.axis_index("col")
    part = lax.rem(col, PLANE)
    half = lax.div(col, PLANE)
    place = half * 4 + row

    def plane_peer(step):
        return (row, half * PLANE + lax.rem(part + step, PLANE))

    def group_peer(step):
        other = lax.rem(place + step, GROUP)
        return (lax.rem(other, 4), lax.div(other, 4) * PLANE + part)

    barrier = pltpu.get_barrier_semaphore()
    for step in (1, 31):
        pl.semaphore_signal(barrier, inc=1, device_id=(row, lax.rem(col + step, 32)), device_id_type=MESH)
    for step in range(1, GROUP):
        pl.semaphore_signal(barrier, inc=1, device_id=group_peer(step), device_id_type=MESH)
    for step in range(1, PLANE):
        pl.semaphore_signal(barrier, inc=1, device_id=plane_peer(step), device_id_type=MESH)

    load = pltpu.make_async_copy(sky_ref, skyx.at[:, HW:HW + 256, :], sky_sem)
    load.start()

    zero = jnp.zeros((512, 256), jnp.bfloat16)
    own = table_ref[HW:HW + 128, :]
    for h in range(2):
        across[h] = zero
        across[h, 0:128, 0:128] = own
        across[h, 128:256, 128:256] = own
        for k in range(2):
            base = HW * (2 * h + k)
            across[h, 256 + base:256 + base + HW, 128 * k:128 * k + 128] = table_ref[0:HW, :]
            across[h, 384 + base:384 + base + HW, 128 * k:128 * k + 128] = table_ref[160:192, :]
    source = lax.broadcasted_iota(jnp.int32, (512, 256), 0)
    target = lax.broadcasted_iota(jnp.int32, (512, 256), 1)
    lane = target % 128
    wanted = (lane // HW) * 128 + lane % HW + jnp.where(target >= 128, 96, 0)
    pick[...] = jnp.where(source == wanted, 1.0, 0.0).astype(jnp.bfloat16)
    down = table_ref[192:256, :]
    grams[...] = jnp.zeros((2, 128, 128), jnp.float32)

    @pl.when(row == 0)
    def _():
        skyx[:, 0:HW, :] = jnp.zeros((CHANS, HW, 128), jnp.bfloat16)

    @pl.when(row == 3)
    def _():
        skyx[:, HW + 256:, :] = jnp.zeros((CHANS, HW, 128), jnp.bfloat16)

    @pl.when(col == 0)
    def _():
        in_l[...] = jnp.zeros(in_l.shape, jnp.bfloat16)

    @pl.when(col == 31)
    def _():
        in_r[...] = jnp.zeros(in_r.shape, jnp.bfloat16)

    pl.semaphore_wait(barrier, PLANE + GROUP)

    to_next = pltpu.make_async_remote_copy(
        src_ref=sky_ref.at[:, 256 - HW:256, :], dst_ref=skyx.at[:, 0:HW, :],
        send_sem=ys.at[0], recv_sem=yr.at[0], device_id=(lax.rem(row + 1, 4), col), device_id_type=MESH)
    to_last = pltpu.make_async_remote_copy(
        src_ref=sky_ref.at[:, 0:HW, :], dst_ref=skyx.at[:, HW + 256:, :],
        send_sem=ys.at[1], recv_sem=yr.at[1], device_id=(lax.rem(row + 3, 4), col), device_id_type=MESH)

    @pl.when(row < 3)
    def _():
        to_next.start()

    @pl.when(row > 0)
    def _():
        to_last.start()

    load.wait()

    def to_right(j):
        return pltpu.make_async_remote_copy(
            src_ref=out_r.at[j], dst_ref=in_l.at[j], send_sem=xs.at[0, j], recv_sem=xr.at[0, j],
            device_id=(row, lax.rem(col + 1, 32)), device_id_type=MESH)

    def to_left(j):
        return pltpu.make_async_remote_copy(
            src_ref=out_l.at[j], dst_ref=in_r.at[j], send_sem=xs.at[1, j], recv_sem=xr.at[1, j],
            device_id=(row, lax.rem(col + 31, 32)), device_id_type=MESH)

    for j in ORDER:
        if j == 0:
            @pl.when(row > 0)
            def _():
                to_next.wait_recv()
        if j == 3:
            @pl.when(row < 3)
            def _():
                to_last.wait_recv()

        def smooth_some(step, carry, j=j):
            c0 = step * 16
            for p in range(8):
                c = c0 + 2 * p
                window = jnp.concatenate(
                    [skyx[c, CHUNK * j:CHUNK * j + 128, :], skyx[c + 1, CHUNK * j:CHUNK * j + 128, :]], axis=1)
                result = jnp.dot(down, window, preferred_element_type=jnp.float32).astype(jnp.bfloat16)
                smooth[j, c] = result[:, 0:128]
                smooth[j, c + 1] = result[:, 128:256]
            return carry

        lax.fori_loop(0, 8, smooth_some, 0)

        def pack_some(step, carry, j=j):
            c0 = step * 32
            wide = jnp.concatenate(
                [smooth[j, pl.ds(c0, 32), 16 * q:16 * q + 16, :].reshape(512, 128) for q in range(4)], axis=1)
            edges = jnp.dot(wide, pick[...], preferred_element_type=jnp.float32).astype(jnp.bfloat16)
            out_l[j, pl.ds(c0, 32)] = edges[:, 0:128].reshape(32, 16, 128)
            out_r[j, pl.ds(c0, 32)] = edges[:, 128:256].reshape(32, 16, 128)
            return carry

        lax.fori_loop(0, 4, pack_some, 0)

        @pl.when(col < 31)
        def _(j=j):
            to_right(j).start()

        @pl.when(col > 0)
        def _(j=j):
            to_left(j).start()

    def put(h, base):
        return pltpu.make_async_copy(stage.at[h], bands_ref.at[pl.ds(base, 32)], stage_sem.at[h])

    for turn, j in enumerate(ORDER):
        @pl.when(col > 0)
        def _(j=j):
            to_right(j).wait_recv()

        @pl.when(col < 31)
        def _(j=j):
            to_left(j).wait_recv()

        for h in range(2):
            def coarse_some(step, carry, j=j, h=h):
                c0 = step * 32
                wide = jnp.concatenate(
                    [smooth[j, pl.ds(c0, 32), 32 * h + 16 * k:32 * h + 16 * k + 16, :].reshape(512, 128)
                     for k in range(2)]
                    + [in_l[j, pl.ds(c0, 32)].reshape(512, 128), in_r[j, pl.ds(c0, 32)].reshape(512, 128)], axis=1)
                both = jnp.dot(wide, across[h], preferred_element_type=jnp.float32)
                both = both.astype(jnp.bfloat16).astype(jnp.float32)
                for k in range(2):
                    begin = HW + CHUNK * j + 32 * h + 16 * k
                    value = both[:, 128 * k:128 * k + 128]
                    pixels = skyx[pl.ds(c0, 32), begin:begin + 16, :].reshape(512, 128).astype(jnp.float32)
                    flat_c[pl.ds(2048 * k + c0 * 16, 512), :] = value
                    flat_f[pl.ds(2048 * k + c0 * 16, 512), :] = pixels - value
                return carry

            lax.fori_loop(0, 4, coarse_some, 0)
            if turn > 0:
                put(h, 0).wait()

            def turn_some(k, carry, h=h):
                for y0 in range(0, 16, 4):
                    for band, flat in ((0, flat_c), (1, flat_f)):
                        lines = []
                        for y in range(y0, y0 + 4):
                            line = flat[pl.ds(2048 * k + y, 128, stride=16), :].astype(jnp.bfloat16)
                            stage[h, 16 * k + y, 128 * band:128 * band + 128, :] = line
                            lines.append(line)
                        wide = jnp.concatenate(lines, axis=1)
                        grams[band] = grams[band] + lax.dot_general(
                            wide, wide, NT, preferred_element_type=jnp.float32)
                return carry

            lax.fori_loop(0, 2, turn_some, 0)
            put(h, CHUNK * j + 32 * h).start()

    for q in range(PLANE):
        pieces[q, 0] = grams[0, 8 * q:8 * q + 8, :]
        pieces[q, 1] = grams[1, 8 * q:8 * q + 8, :]
        pieces[q, 2] = flag_ref[...]
    one = []
    for step in range(1, PLANE):
        one.append(pltpu.make_async_remote_copy(
            src_ref=pieces.at[lax.rem(part + step, PLANE)], dst_ref=first.at[step],
            send_sem=s1.at[step], recv_sem=r1.at[step],
            device_id=plane_peer(step), device_id_type=MESH))
    for copy in one:
        copy.start()
    first[0] = pieces[part]
    for copy in one:
        copy.wait_recv()
    for region in range(8):
        total0 = jnp.zeros((8, 128), jnp.float32)
        total1 = jnp.zeros((8, 128), jnp.float32)
        for step in range(PLANE):
            flag = first[step, 2, region:region + 1, :]
            total0 = total0 + flag * first[step, 0]
            total1 = total1 + flag * first[step, 1]
        slots[region, 0] = total0
        slots[region, 1] = total1

    two = []
    for step in range(1, GROUP):
        two.append(pltpu.make_async_remote_copy(
            src_ref=slots, dst_ref=others.at[step],
            send_sem=s2.at[step], recv_sem=r2.at[step],
            device_id=group_peer(step), device_id_type=MESH))
    for copy in two:
        copy.start()
    for copy in two:
        copy.wait_recv()
    sums = []
    for region in range(8):
        pair = []
        for band in range(2):
            total = slots[region, band]
            for step in range(1, GROUP):
                total = total + others[step, region, band]
            pair.append(total)
        sums.append(pair)

    for step in range(PLANE):
        for band in range(2):
            total = jnp.zeros((8, 128), jnp.float32)
            for region in range(8):
                total = total + first[step, 2, region:region + 1, :] * sums[region][band]
            picked[step, band] = total
    three = []
    for step in range(1, PLANE):
        back = lax.rem(part + PLANE - step, PLANE)
        three.append(pltpu.make_async_remote_copy(
            src_ref=picked.at[step], dst_ref=last.at[part],
            send_sem=s3.at[step], recv_sem=r3.at[step],
            device_id=(row, half * PLANE + back), device_id_type=MESH))
    for copy in three:
        copy.start()
    last[part] = picked[0]
    for step in range(1, PLANE):
        ahead = lax.rem(part + step, PLANE)
        pltpu.make_async_remote_copy(
            src_ref=picked.at[step], dst_ref=last.at[ahead],
            send_sem=s3.at[step], recv_sem=r3.at[step],
            device_id=(row, half * PLANE + ahead), device_id_type=MESH).wait_recv()
    for index in range(PLANE):
        for band in range(2):
            gram_ref[band, index * 8:index * 8 + 8, :] = last[index, band]

    for h in range(2):
        put(h, 0).wait()

    @pl.when(row < 3)
    def _():
        to_next.wait_send()

    @pl.when(row > 0)
    def _():
        to_last.wait_send()

    @pl.when(col < 31)
    def _():
        for j in ORDER:
            to_right(j).wait_send()

    @pl.when(col > 0)
    def _():
        for j in ORDER:
            to_left(j).wait_send()

    for copy in one + two + three:
        copy.wait_send()


def front(sky, table, flags):
    bf, f32 = jnp.bfloat16, jnp.float32
    dma = pltpu.SemaphoreType.DMA
    return pl.pallas_call(
        front_kernel,
        out_shape=(jax.ShapeDtypeStruct((256, 256, 128), bf), jax.ShapeDtypeStruct((2, 128, 128), f32)),
        in_specs=[pl.BlockSpec(memory_space=pl.ANY)] + [pl.BlockSpec(memory_space=pltpu.VMEM)] * 2,
        out_specs=(pl.BlockSpec(memory_space=pl.ANY), pl.BlockSpec(memory_space=pltpu.VMEM)),
        scratch_shapes=[
            pltpu.VMEM((CHANS, 256 + 2 * HW, 128), bf),
            pltpu.VMEM((4, CHANS, CHUNK, 128), bf),
            pltpu.VMEM((4, CHANS, 16, 128), bf),
            pltpu.VMEM((4, CHANS, 16, 128), bf),
            pltpu.VMEM((4, CHANS, 16, 128), bf),
            pltpu.VMEM((4, CHANS, 16, 128), bf),
            pltpu.VMEM((2, 512, 256), bf),
            pltpu.VMEM((512, 256), bf),
            pltpu.VMEM((4096, 128), f32),
            pltpu.VMEM((4096, 128), f32),
            pltpu.VMEM((2, 32, 256, 128), bf),
            pltpu.VMEM((2, 128, 128), f32),
            pltpu.VMEM((PLANE, 3, 8, 128), f32),
            pltpu.VMEM((PLANE, 3, 8, 128), f32),
            pltpu.VMEM((8, 2, 8, 128), f32),
            pltpu.VMEM((GROUP, 8, 2, 8, 128), f32),
            pltpu.VMEM((PLANE, 2, 8, 128), f32),
            pltpu.VMEM((PLANE, 2, 8, 128), f32),
            dma, dma((2,)), dma((2,)), dma((2, 4)), dma((2, 4)), dma((2,)),
            dma((PLANE,)), dma((PLANE,)), dma((GROUP,)), dma((GROUP,)), dma((PLANE,)), dma((PLANE,)),
        ],
        compiler_params=pltpu.CompilerParams(
            collective_id=1, has_side_effects=True, vmem_limit_bytes=56 * 1024 * 1024),
        name="front",
    )(sky, table, flags)


def weights_of(grams, priors, cheb_t, keep):
    lanes = lax.broadcasted_iota(jnp.int32, (8, 128), 1)
    subs = lax.broadcasted_iota(jnp.int32, (8, 128), 0)
    mats = []
    for band in range(2):
        blocks = []
        for i in range(16):
            block = grams[band][i * 8:i * 8 + 8, :]
            diag = jnp.where(lanes == subs + 8 * i, priors[band], 0.0)
            blocks.append(block / 524288.0 + diag)
        blocks.append(cheb_t)
        mats.append(blocks)
    for k in range(128):
        at, off = k // 8, k % 8
        hit = lanes[0:1, :] == k
        for band in range(2):
            m = mats[band]
            cols = [jnp.broadcast_to(b[:, k:k + 1], (8, 128)) for b in m]
            inv = 1.0 / cols[at][off:off + 1, :]
            line = m[at][off:off + 1, :] * inv
            line = jnp.where(hit, 1.0 - inv, line)
            mats[band] = [b - c * line for b, c in zip(m, cols)]
    out = []
    for band in range(2):
        mixed = mats[band][16] * keep
        kept = cheb_t * keep
        small = lax.dot_general(kept, mixed, (((1,), (1,)), ((), ())), precision=HIGH,
                                preferred_element_type=jnp.float32)
        eye = (lax.broadcasted_iota(jnp.int32, (8, 8), 0) == lax.broadcasted_iota(jnp.int32, (8, 8), 1))
        small = small + jnp.where(eye, 1.0 - keep[:, 0:8], 0.0)
        out.append((small, mixed))
    weights = []
    for small, mixed in out:
        for k in range(8):
            fac = small[:, k:k + 1]
            inv = 1.0 / fac[k:k + 1, :]
            shift = jnp.where(subs[:, 0:1] == k, 1.0, 0.0)
            fac = fac - shift
            srow = small[k:k + 1, :] * inv
            mrow = mixed[k:k + 1, :] * inv
            small = small - fac * srow
            mixed = mixed - fac * mrow
        weights.append(mixed)
    return weights


def back_kernel(gram_ref, prior_ref, cheb_ref, keep_ref, bands_ref, out_ref, proj, flat):
    @pl.when(pl.program_id(0) == 0)
    def _():
        cheb_t = cheb_ref[...]
        keep = keep_ref[...]
        weights = weights_of([gram_ref[0], gram_ref[1]], [prior_ref[0:1, :], prior_ref[1:2, :]], cheb_t, keep)
        kept = cheb_t * keep
        for band in range(2):
            part = lax.dot_general(kept, weights[band], (((0,), (0,)), ((), ())), precision=HIGH,
                                   preferred_element_type=jnp.float32)
            proj[:, 128 * band:128 * band + 128] = part.astype(jnp.bfloat16)

    for y in range(0, 16, 2):
        pair = jnp.concatenate([bands_ref[y], bands_ref[y + 1]], axis=1)
        removed = jnp.dot(proj[...], pair, preferred_element_type=jnp.float32)
        wide = pair.astype(jnp.float32)
        result = wide[0:128] + wide[128:256] - removed
        flat[pl.ds(y, 128, stride=16), :] = result[:, 0:128]
        flat[pl.ds(y + 1, 128, stride=16), :] = result[:, 128:256]
    out_ref[...] = flat[...].reshape(128, 16, 128).astype(jnp.bfloat16)


def back(grams, prior_var, cheb_t, keep, bands):
    whole = pl.BlockSpec(memory_space=pltpu.VMEM)
    return pl.pallas_call(
        back_kernel,
        grid=(16,),
        out_shape=jax.ShapeDtypeStruct((128, 256, 128), jnp.bfloat16),
        in_specs=[whole] * 4 + [pl.BlockSpec((16, 256, 128), lambda i: (i, 0, 0))],
        out_specs=pl.BlockSpec((128, 16, 128), lambda i: (0, i, 0)),
        scratch_shapes=[pltpu.VMEM((128, 256), jnp.bfloat16), pltpu.VMEM((2048, 128), jnp.float32)],
        name="back",
    )(grams, prior_var, cheb_t, keep, bands)


def taps_table(kernel_widths):
    line = lax.broadcasted_iota(jnp.int32, (256, 128), 0)
    lane = lax.broadcasted_iota(jnp.int32, (256, 128), 1)
    first = line < 192
    offsets = jnp.where(first, line - lane - HW, lane - (line - 192) - HW).astype(jnp.float32)
    spread = jnp.where(first, kernel_widths[1], kernel_widths[0]).astype(jnp.float32)
    values = (1.0 + jnp.cos(math.pi * offsets / (spread + 1.0))) / (2.0 * spread + 2.0)
    return jnp.where(jnp.abs(offsets) <= spread, values, 0.0).astype(jnp.bfloat16)


def chebyshev_rows(chan_count, degree):
    position = (2.0 * jnp.arange(chan_count, dtype=jnp.float32) + 1.0) / chan_count - 1.0
    terms = [jnp.ones_like(position), position]
    for order in range(2, degree):
        terms.append(2.0 * position * terms[-1] - terms[-2])
    return jnp.stack(terms[:degree], axis=0)


def local(sky, kernel_widths, prior_var, tile_region, region_rank):
    region = tile_region[0, 0]
    flags = jnp.broadcast_to((jnp.arange(8) == region).astype(jnp.float32)[:, None], (8, 128))
    keep_rank = lax.dynamic_index_in_dim(region_rank, region, 0, keepdims=False)
    keep = jnp.broadcast_to((jnp.arange(8) < keep_rank).astype(jnp.float32)[:, None], (8, 128))
    bands, own_gram = front(sky, taps_table(kernel_widths), flags)
    return back(own_gram, prior_var, chebyshev_rows(sky.shape[0], MMAX), keep, bands)


def solution(mesh):
    return jax.shard_map(
        local,
        mesh=mesh,
        in_specs=(P(None, "row", "col"), P(), P(), P("row", "col"), P()),
        out_specs=P(None, "row", "col"),
        check_vma=False,
    )
```

```python
import math
import jax
import jax.numpy as jnp
from jax import lax
from jax.experimental import pallas as pl
from jax.experimental.pallas import tpu as pltpu
from jax.sharding import PartitionSpec as P

HW = 32
MMAX = 8
TPR = 16
PLANE = 16
GROUP = 8
CHANS = 128
CHUNK = 64
ORDER = (1, 2, 0, 3)
MESH = pl.DeviceIdType.MESH
HIGH = lax.Precision.HIGHEST
NT = (((1,), (1,)), ((), ()))


def taps_table(down_width, across_width):
    line = lax.broadcasted_iota(jnp.int32, (256, 128), 0)
    lane = lax.broadcasted_iota(jnp.int32, (256, 128), 1)
    first = line < 192
    offsets = jnp.where(first, line - lane - HW, lane - (line - 192) - HW).astype(jnp.float32)
    spread = jnp.where(first, across_width, down_width).astype(jnp.float32)
    values = (1.0 + jnp.cos(math.pi * offsets / (spread + 1.0))) / (2.0 * spread + 2.0)
    return jnp.where(jnp.abs(offsets) <= spread, values, 0.0).astype(jnp.bfloat16)


def front_kernel(widths_ref, region_ref, sky_ref, bands_ref, gram_ref,
                 table_ref, skyx, smooth, out_l, out_r, in_l, in_r, across, pick, flat_c, flat_f, stage, grams, pieces,
                 first, slots, others, picked, last,
                 go, sky_sem, ys, yr, xs, xr, stage_sem, s1, r1, s2, r2, s3, r3):
    row = lax.axis_index("row")
    col = lax.axis_index("col")
    part = lax.rem(col, PLANE)
    half = lax.div(col, PLANE)
    place = half * 4 + row

    def plane_peer(step):
        return (row, half * PLANE + lax.rem(part + step, PLANE))

    def group_peer(step):
        other = lax.rem(place + step, GROUP)
        return (lax.rem(other, 4), lax.div(other, 4) * PLANE + part)

    barrier = pltpu.get_barrier_semaphore()
    for step in (1, 31):
        pl.semaphore_signal(barrier, inc=1, device_id=(row, lax.rem(col + step, 32)), device_id_type=MESH)
    for step in range(1, GROUP):
        pl.semaphore_signal(barrier, inc=1, device_id=group_peer(step), device_id_type=MESH)
    for step in range(1, PLANE):
        pl.semaphore_signal(barrier, inc=1, device_id=plane_peer(step), device_id_type=MESH)

    load = pltpu.make_async_copy(sky_ref, skyx.at[:, HW:HW + 256, :], sky_sem)
    load.start()

    table_ref[...] = taps_table(widths_ref[0], widths_ref[1])

    zero = jnp.zeros((512, 256), jnp.bfloat16)
    own = table_ref[HW:HW + 128, :]
    for h in range(2):
        across[h] = zero
        across[h, 0:128, 0:128] = own
        across[h, 128:256, 128:256] = own
        for k in range(2):
            base = HW * (2 * h + k)
            across[h, 256 + base:256 + base + HW, 128 * k:128 * k + 128] = table_ref[0:HW, :]
            across[h, 384 + base:384 + base + HW, 128 * k:128 * k + 128] = table_ref[160:192, :]
    source = lax.broadcasted_iota(jnp.int32, (512, 256), 0)
    target = lax.broadcasted_iota(jnp.int32, (512, 256), 1)
    lane = target % 128
    wanted = (lane // HW) * 128 + lane % HW + jnp.where(target >= 128, 96, 0)
    pick[...] = jnp.where(source == wanted, 1.0, 0.0).astype(jnp.bfloat16)
    down = table_ref[192:256, :]
    grams[...] = jnp.zeros((2, 128, 128), jnp.float32)

    @pl.when(row == 0)
    def _():
        skyx[:, 0:HW, :] = jnp.zeros((CHANS, HW, 128), jnp.bfloat16)

    @pl.when(row == 3)
    def _():
        skyx[:, HW + 256:, :] = jnp.zeros((CHANS, HW, 128), jnp.bfloat16)

    @pl.when(col == 0)
    def _():
        in_l[...] = jnp.zeros(in_l.shape, jnp.bfloat16)

    @pl.when(col == 31)
    def _():
        in_r[...] = jnp.zeros(in_r.shape, jnp.bfloat16)

    pl.semaphore_wait(barrier, PLANE + GROUP)

    to_next = pltpu.make_async_remote_copy(
        src_ref=sky_ref.at[:, 256 - HW:256, :], dst_ref=skyx.at[:, 0:HW, :],
        send_sem=ys.at[0], recv_sem=yr.at[0], device_id=(lax.rem(row + 1, 4), col), device_id_type=MESH)
    to_last = pltpu.make_async_remote_copy(
        src_ref=sky_ref.at[:, 0:HW, :], dst_ref=skyx.at[:, HW + 256:, :],
        send_sem=ys.at[1], recv_sem=yr.at[1], device_id=(lax.rem(row + 3, 4), col), device_id_type=MESH)

    @pl.when(row < 3)
    def _():
        to_next.start()

    @pl.when(row > 0)
    def _():
        to_last.start()

    load.wait()

    def to_right(j):
        return pltpu.make_async_remote_copy(
            src_ref=out_r.at[j], dst_ref=in_l.at[j], send_sem=xs.at[0, j], recv_sem=xr.at[0, j],
            device_id=(row, lax.rem(col + 1, 32)), device_id_type=MESH)

    def to_left(j):
        return pltpu.make_async_remote_copy(
            src_ref=out_l.at[j], dst_ref=in_r.at[j], send_sem=xs.at[1, j], recv_sem=xr.at[1, j],
            device_id=(row, lax.rem(col + 31, 32)), device_id_type=MESH)

    for j in ORDER:
        if j == ORDER[2]:
            @pl.when(row > 0)
            def _():
                to_next.wait_recv()

            @pl.when(row < 3)
            def _():
                to_last.wait_recv()

            middle = (row == 1) | (row == 2)
            crossing = (col == 15) | (col == 16)

            @pl.when(middle & (col == 12))
            def _():
                pl.semaphore_signal(go, inc=1, device_id=(row, col + 3), device_id_type=MESH)

            @pl.when(middle & (col == 19))
            def _():
                pl.semaphore_signal(go, inc=1, device_id=(row, col - 3), device_id_type=MESH)

            @pl.when(crossing)
            def _():
                pl.semaphore_wait(go, 1)

            @pl.when(middle & crossing)
            def _():
                pl.semaphore_signal(go, inc=1, device_id=((row - 1) * 3, col), device_id_type=MESH)

            @pl.when(col == 15)
            def _():
                to_right(ORDER[0]).start()
                to_right(ORDER[1]).start()

            @pl.when(col == 16)
            def _():
                to_left(ORDER[0]).start()
                to_left(ORDER[1]).start()

        def smooth_some(step, carry, j=j):
            c0 = step * 16
            for p in range(8):
                c = c0 + 2 * p
                window = jnp.concatenate(
                    [skyx[c, CHUNK * j:CHUNK * j + 128, :], skyx[c + 1, CHUNK * j:CHUNK * j + 128, :]], axis=1)
                result = jnp.dot(down, window, preferred_element_type=jnp.float32).astype(jnp.bfloat16)
                smooth[j, c] = result[:, 0:128]
                smooth[j, c + 1] = result[:, 128:256]
            return carry

        lax.fori_loop(0, 8, smooth_some, 0)

        def pack_some(step, carry, j=j):
            c0 = step * 32
            wide = jnp.concatenate(
                [smooth[j, pl.ds(c0, 32), 16 * q:16 * q + 16, :].reshape(512, 128) for q in range(4)], axis=1)
            edges = jnp.dot(wide, pick[...], preferred_element_type=jnp.float32).astype(jnp.bfloat16)
            out_l[j, pl.ds(c0, 32)] = edges[:, 0:128].reshape(32, 16, 128)
            out_r[j, pl.ds(c0, 32)] = edges[:, 128:256].reshape(32, 16, 128)
            return carry

        lax.fori_loop(0, 4, pack_some, 0)

        late = j in ORDER[2:]

        @pl.when((col < 31) & (late | (col != 15)))
        def _(j=j):
            to_right(j).start()

        @pl.when((col > 0) & (late | (col != 16)))
        def _(j=j):
            to_left(j).start()

    def put(h, base):
        return pltpu.make_async_copy(stage.at[h], bands_ref.at[pl.ds(base, 32)], stage_sem.at[h])

    for turn, j in enumerate(ORDER):
        @pl.when(col > 0)
        def _(j=j):
            to_right(j).wait_recv()

        @pl.when(col < 31)
        def _(j=j):
            to_left(j).wait_recv()

        for h in range(2):
            def coarse_some(step, carry, j=j, h=h):
                c0 = step * 32
                wide = jnp.concatenate(
                    [smooth[j, pl.ds(c0, 32), 32 * h + 16 * k:32 * h + 16 * k + 16, :].reshape(512, 128)
                     for k in range(2)]
                    + [in_l[j, pl.ds(c0, 32)].reshape(512, 128), in_r[j, pl.ds(c0, 32)].reshape(512, 128)], axis=1)
                both = jnp.dot(wide, across[h], preferred_element_type=jnp.float32)
                both = both.astype(jnp.bfloat16).astype(jnp.float32)
                for k in range(2):
                    begin = HW + CHUNK * j + 32 * h + 16 * k
                    value = both[:, 128 * k:128 * k + 128]
                    pixels = skyx[pl.ds(c0, 32), begin:begin + 16, :].reshape(512, 128).astype(jnp.float32)
                    flat_c[pl.ds(2048 * k + c0 * 16, 512), :] = value
                    flat_f[pl.ds(2048 * k + c0 * 16, 512), :] = pixels - value
                return carry

            lax.fori_loop(0, 4, coarse_some, 0)
            if turn > 0:
                put(h, 0).wait()

            def turn_some(k, carry, h=h):
                for y0 in range(0, 16, 4):
                    for band, flat in ((0, flat_c), (1, flat_f)):
                        lines = []
                        for y in range(y0, y0 + 4):
                            line = flat[pl.ds(2048 * k + y, 128, stride=16), :].astype(jnp.bfloat16)
                            stage[h, 16 * k + y, 128 * band:128 * band + 128, :] = line
                            lines.append(line)
                        wide = jnp.concatenate(lines, axis=1)
                        grams[band] = grams[band] + lax.dot_general(
                            wide, wide, NT, preferred_element_type=jnp.float32)
                return carry

            lax.fori_loop(0, 2, turn_some, 0)
            put(h, CHUNK * j + 32 * h).start()

    flag = jnp.where(lax.broadcasted_iota(jnp.int32, (8, 128), 0) == region_ref[0, 0], 1.0, 0.0)
    for q in range(PLANE):
        pieces[q, 0] = grams[0, 8 * q:8 * q + 8, :]
        pieces[q, 1] = grams[1, 8 * q:8 * q + 8, :]
        pieces[q, 2] = flag
    one = []
    for step in range(1, PLANE):
        one.append(pltpu.make_async_remote_copy(
            src_ref=pieces.at[lax.rem(part + step, PLANE)], dst_ref=first.at[step],
            send_sem=s1.at[step], recv_sem=r1.at[step],
            device_id=plane_peer(step), device_id_type=MESH))
    for copy in one:
        copy.start()
    first[0] = pieces[part]
    for copy in one:
        copy.wait_recv()
    for region in range(8):
        total0 = jnp.zeros((8, 128), jnp.float32)
        total1 = jnp.zeros((8, 128), jnp.float32)
        for step in range(PLANE):
            flag = first[step, 2, region:region + 1, :]
            total0 = total0 + flag * first[step, 0]
            total1 = total1 + flag * first[step, 1]
        slots[region, 0] = total0
        slots[region, 1] = total1

    two = []
    for step in range(1, GROUP):
        two.append(pltpu.make_async_remote_copy(
            src_ref=slots, dst_ref=others.at[step],
            send_sem=s2.at[step], recv_sem=r2.at[step],
            device_id=group_peer(step), device_id_type=MESH))
    for copy in two:
        copy.start()
    for copy in two:
        copy.wait_recv()
    sums = []
    for region in range(8):
        pair = []
        for band in range(2):
            total = slots[region, band]
            for step in range(1, GROUP):
                total = total + others[step, region, band]
            pair.append(total)
        sums.append(pair)

    for step in range(PLANE):
        for band in range(2):
            total = jnp.zeros((8, 128), jnp.float32)
            for region in range(8):
                total = total + first[step, 2, region:region + 1, :] * sums[region][band]
            picked[step, band] = total
    three = []
    for step in range(1, PLANE):
        back = lax.rem(part + PLANE - step, PLANE)
        three.append(pltpu.make_async_remote_copy(
            src_ref=picked.at[step], dst_ref=last.at[part],
            send_sem=s3.at[step], recv_sem=r3.at[step],
            device_id=(row, half * PLANE + back), device_id_type=MESH))
    for copy in three:
        copy.start()
    last[part] = picked[0]
    for step in range(1, PLANE):
        ahead = lax.rem(part + step, PLANE)
        pltpu.make_async_remote_copy(
            src_ref=picked.at[step], dst_ref=last.at[ahead],
            send_sem=s3.at[step], recv_sem=r3.at[step],
            device_id=(row, half * PLANE + ahead), device_id_type=MESH).wait_recv()
    for index in range(PLANE):
        for band in range(2):
            gram_ref[band, index * 8:index * 8 + 8, :] = last[index, band]

    for h in range(2):
        put(h, 0).wait()

    @pl.when(row < 3)
    def _():
        to_next.wait_send()

    @pl.when(row > 0)
    def _():
        to_last.wait_send()

    @pl.when(col < 31)
    def _():
        for j in ORDER:
            to_right(j).wait_send()

    @pl.when(col > 0)
    def _():
        for j in ORDER:
            to_left(j).wait_send()

    for copy in one + two + three:
        copy.wait_send()


def front(widths, region, sky):
    bf, f32 = jnp.bfloat16, jnp.float32
    dma = pltpu.SemaphoreType.DMA
    return pl.pallas_call(
        front_kernel,
        out_shape=(jax.ShapeDtypeStruct((256, 256, 128), bf), jax.ShapeDtypeStruct((2, 128, 128), f32)),
        in_specs=[pl.BlockSpec(memory_space=pltpu.SMEM)] * 2 + [pl.BlockSpec(memory_space=pl.ANY)],
        out_specs=(pl.BlockSpec(memory_space=pl.ANY), pl.BlockSpec(memory_space=pltpu.VMEM)),
        scratch_shapes=[
            pltpu.VMEM((256, 128), bf),
            pltpu.VMEM((CHANS, 256 + 2 * HW, 128), bf),
            pltpu.VMEM((4, CHANS, CHUNK, 128), bf),
            pltpu.VMEM((4, CHANS, 16, 128), bf),
            pltpu.VMEM((4, CHANS, 16, 128), bf),
            pltpu.VMEM((4, CHANS, 16, 128), bf),
            pltpu.VMEM((4, CHANS, 16, 128), bf),
            pltpu.VMEM((2, 512, 256), bf),
            pltpu.VMEM((512, 256), bf),
            pltpu.VMEM((4096, 128), f32),
            pltpu.VMEM((4096, 128), f32),
            pltpu.VMEM((2, 32, 256, 128), bf),
            pltpu.VMEM((2, 128, 128), f32),
            pltpu.VMEM((PLANE, 3, 8, 128), f32),
            pltpu.VMEM((PLANE, 3, 8, 128), f32),
            pltpu.VMEM((8, 2, 8, 128), f32),
            pltpu.VMEM((GROUP, 8, 2, 8, 128), f32),
            pltpu.VMEM((PLANE, 2, 8, 128), f32),
            pltpu.VMEM((PLANE, 2, 8, 128), f32),
            pltpu.SemaphoreType.REGULAR,
            dma, dma((2,)), dma((2,)), dma((2, 4)), dma((2, 4)), dma((2,)),
            dma((PLANE,)), dma((PLANE,)), dma((GROUP,)), dma((GROUP,)), dma((PLANE,)), dma((PLANE,)),
        ],
        compiler_params=pltpu.CompilerParams(
            collective_id=1, has_side_effects=True, vmem_limit_bytes=56 * 1024 * 1024),
        name="front",
    )(widths, region, sky)


def weights_of(grams, priors, cheb_t, keep):
    lanes = lax.broadcasted_iota(jnp.int32, (8, 128), 1)
    subs = lax.broadcasted_iota(jnp.int32, (8, 128), 0)
    mats = []
    for band in range(2):
        blocks = []
        for i in range(16):
            block = grams[band][i * 8:i * 8 + 8, :]
            diag = jnp.where(lanes == subs + 8 * i, priors[band], 0.0)
            blocks.append(block / 524288.0 + diag)
        blocks.append(cheb_t)
        mats.append(blocks)
    for k in range(128):
        at, off = k // 8, k % 8
        hit = lanes[0:1, :] == k
        for band in range(2):
            m = mats[band]
            cols = [jnp.broadcast_to(b[:, k:k + 1], (8, 128)) for b in m]
            inv = 1.0 / cols[at][off:off + 1, :]
            line = m[at][off:off + 1, :] * inv
            line = jnp.where(hit, 1.0 - inv, line)
            mats[band] = [b - c * line for b, c in zip(m, cols)]
    out = []
    for band in range(2):
        mixed = mats[band][16] * keep
        kept = cheb_t * keep
        small = lax.dot_general(kept, mixed, (((1,), (1,)), ((), ())), precision=HIGH,
                                preferred_element_type=jnp.float32)
        eye = (lax.broadcasted_iota(jnp.int32, (8, 8), 0) == lax.broadcasted_iota(jnp.int32, (8, 8), 1))
        small = small + jnp.where(eye, 1.0 - keep[:, 0:8], 0.0)
        out.append((small, mixed))
    weights = []
    for small, mixed in out:
        for k in range(8):
            fac = small[:, k:k + 1]
            inv = 1.0 / fac[k:k + 1, :]
            shift = jnp.where(subs[:, 0:1] == k, 1.0, 0.0)
            fac = fac - shift
            srow = small[k:k + 1, :] * inv
            mrow = mixed[k:k + 1, :] * inv
            small = small - fac * srow
            mixed = mixed - fac * mrow
        weights.append(mixed)
    return weights


def chebyshev_rows():
    lane = lax.broadcasted_iota(jnp.int32, (8, 128), 1).astype(jnp.float32)
    order = lax.broadcasted_iota(jnp.int32, (8, 128), 0)
    position = (2.0 * lane + 1.0) / CHANS - 1.0
    terms = [jnp.ones_like(position), position]
    rows = jnp.where(order == 0, terms[0], position)
    for m in range(2, MMAX):
        terms.append(2.0 * position * terms[-1] - terms[-2])
        rows = jnp.where(order == m, terms[-1], rows)
    return rows


def back_kernel(region_ref, rank_ref, gram_ref, prior_ref, bands_ref, out_ref, proj, flat):
    @pl.when(pl.program_id(0) == 0)
    def _():
        cheb_t = chebyshev_rows()
        rank = rank_ref[region_ref[0, 0]]
        keep = jnp.where(lax.broadcasted_iota(jnp.int32, (8, 128), 0) < rank, 1.0, 0.0)
        weights = weights_of([gram_ref[0], gram_ref[1]], [prior_ref[0:1, :], prior_ref[1:2, :]], cheb_t, keep)
        kept = cheb_t * keep
        for band in range(2):
            part = lax.dot_general(kept, weights[band], (((0,), (0,)), ((), ())), precision=HIGH,
                                   preferred_element_type=jnp.float32)
            proj[:, 128 * band:128 * band + 128] = part.astype(jnp.bfloat16)

    for y in range(0, 16, 2):
        pair = jnp.concatenate([bands_ref[y], bands_ref[y + 1]], axis=1)
        removed = jnp.dot(proj[...], pair, preferred_element_type=jnp.float32)
        wide = pair.astype(jnp.float32)
        result = wide[0:128] + wide[128:256] - removed
        flat[pl.ds(y, 128, stride=16), :] = result[:, 0:128]
        flat[pl.ds(y + 1, 128, stride=16), :] = result[:, 128:256]
    out_ref[...] = flat[...].reshape(128, 16, 128).astype(jnp.bfloat16)


def back(region, ranks, grams, prior_var, bands):
    whole = pl.BlockSpec(memory_space=pltpu.VMEM)
    return pl.pallas_call(
        back_kernel,
        grid=(16,),
        out_shape=jax.ShapeDtypeStruct((128, 256, 128), jnp.bfloat16),
        in_specs=[pl.BlockSpec(memory_space=pltpu.SMEM)] * 2 + [whole] * 2 + [pl.BlockSpec((16, 256, 128), lambda i: (i, 0, 0))],
        out_specs=pl.BlockSpec((128, 16, 128), lambda i: (0, i, 0)),
        scratch_shapes=[pltpu.VMEM((128, 256), jnp.bfloat16), pltpu.VMEM((2048, 128), jnp.float32)],
        name="back",
    )(region, ranks, grams, prior_var, bands)


def local(sky, kernel_widths, prior_var, tile_region, region_rank):
    bands, own_gram = front(kernel_widths, tile_region, sky)
    return back(tile_region, region_rank, own_gram, prior_var, bands)


def solution(mesh):
    return jax.shard_map(
        local,
        mesh=mesh,
        in_specs=(P(None, "row", "col"), P(), P(), P("row", "col"), P()),
        out_specs=P(None, "row", "col"),
        check_vma=False,
    )
```

```python
import math
import jax
import jax.numpy as jnp
from jax import lax
from jax.experimental import pallas as pl
from jax.experimental.pallas import tpu as pltpu
from jax.sharding import PartitionSpec as P

HW = 32
MMAX = 8
TPR = 16
PLANE = 16
GROUP = 8
CHANS = 128
CHUNK = 64
ORDER = (1, 2, 0, 3)
MESH = pl.DeviceIdType.MESH
HIGH = lax.Precision.HIGHEST
NT = (((1,), (1,)), ((), ()))


def taps_table(down_width, across_width):
    line = lax.broadcasted_iota(jnp.int32, (256, 128), 0)
    lane = lax.broadcasted_iota(jnp.int32, (256, 128), 1)
    first = line < 192
    offsets = jnp.where(first, line - lane - HW, lane - (line - 192) - HW).astype(jnp.float32)
    spread = jnp.where(first, across_width, down_width).astype(jnp.float32)
    values = (1.0 + jnp.cos(math.pi * offsets / (spread + 1.0))) / (2.0 * spread + 2.0)
    return jnp.where(jnp.abs(offsets) <= spread, values, 0.0).astype(jnp.bfloat16)


def front_kernel(widths_ref, region_ref, sky_ref, bands_ref, gram_ref,
                 table_ref, skyx, smooth, out_l, out_r, in_l, in_r, across, pick, flat_c, flat_f, grams, pieces,
                 first, slots, others, picked, last,
                 go, sky_sem, ys, yr, xs, xr, s1, r1, s2, r2, s3, r3):
    row = lax.axis_index("row")
    col = lax.axis_index("col")
    part = lax.rem(col, PLANE)
    half = lax.div(col, PLANE)
    place = half * 4 + row

    def plane_peer(step):
        return (row, half * PLANE + lax.rem(part + step, PLANE))

    def group_peer(step):
        other = lax.rem(place + step, GROUP)
        return (lax.rem(other, 4), lax.div(other, 4) * PLANE + part)

    barrier = pltpu.get_barrier_semaphore()
    for step in (1, 31):
        pl.semaphore_signal(barrier, inc=1, device_id=(row, lax.rem(col + step, 32)), device_id_type=MESH)
    for step in range(1, GROUP):
        pl.semaphore_signal(barrier, inc=1, device_id=group_peer(step), device_id_type=MESH)
    for step in range(1, PLANE):
        pl.semaphore_signal(barrier, inc=1, device_id=plane_peer(step), device_id_type=MESH)

    load = pltpu.make_async_copy(sky_ref, skyx.at[:, HW:HW + 256, :], sky_sem)
    load.start()

    table_ref[...] = taps_table(widths_ref[0], widths_ref[1])

    zero = jnp.zeros((512, 256), jnp.bfloat16)
    own = table_ref[HW:HW + 128, :]
    for h in range(2):
        across[h] = zero
        across[h, 0:128, 0:128] = own
        across[h, 128:256, 128:256] = own
        for k in range(2):
            base = HW * (2 * h + k)
            across[h, 256 + base:256 + base + HW, 128 * k:128 * k + 128] = table_ref[0:HW, :]
            across[h, 384 + base:384 + base + HW, 128 * k:128 * k + 128] = table_ref[160:192, :]
    source = lax.broadcasted_iota(jnp.int32, (512, 256), 0)
    target = lax.broadcasted_iota(jnp.int32, (512, 256), 1)
    lane = target % 128
    wanted = (lane // HW) * 128 + lane % HW + jnp.where(target >= 128, 96, 0)
    pick[...] = jnp.where(source == wanted, 1.0, 0.0).astype(jnp.bfloat16)
    down = table_ref[192:256, :]
    grams[...] = jnp.zeros((2, 128, 128), jnp.float32)

    @pl.when(row == 0)
    def _():
        skyx[:, 0:HW, :] = jnp.zeros((CHANS, HW, 128), jnp.bfloat16)

    @pl.when(row == 3)
    def _():
        skyx[:, HW + 256:, :] = jnp.zeros((CHANS, HW, 128), jnp.bfloat16)

    @pl.when(col == 0)
    def _():
        in_l[...] = jnp.zeros(in_l.shape, jnp.bfloat16)

    @pl.when(col == 31)
    def _():
        in_r[...] = jnp.zeros(in_r.shape, jnp.bfloat16)

    to_next = pltpu.make_async_remote_copy(
        src_ref=sky_ref.at[:, 256 - HW:256, :], dst_ref=skyx.at[:, 0:HW, :],
        send_sem=ys.at[0], recv_sem=yr.at[0], device_id=(lax.rem(row + 1, 4), col), device_id_type=MESH)
    to_last = pltpu.make_async_remote_copy(
        src_ref=sky_ref.at[:, 0:HW, :], dst_ref=skyx.at[:, HW + 256:, :],
        send_sem=ys.at[1], recv_sem=yr.at[1], device_id=(lax.rem(row + 3, 4), col), device_id_type=MESH)

    def to_right(j):
        return pltpu.make_async_remote_copy(
            src_ref=out_r.at[j], dst_ref=in_l.at[j], send_sem=xs.at[0, j], recv_sem=xr.at[0, j],
            device_id=(row, lax.rem(col + 1, 32)), device_id_type=MESH)

    def to_left(j):
        return pltpu.make_async_remote_copy(
            src_ref=out_l.at[j], dst_ref=in_r.at[j], send_sem=xs.at[1, j], recv_sem=xr.at[1, j],
            device_id=(row, lax.rem(col + 31, 32)), device_id_type=MESH)

    def smooth_chunk(j):
        def smooth_some(step, carry):
            c0 = step * 16
            for p in range(8):
                c = c0 + 2 * p
                window = jnp.concatenate(
                    [skyx[c, CHUNK * j:CHUNK * j + 128, :], skyx[c + 1, CHUNK * j:CHUNK * j + 128, :]], axis=1)
                result = jnp.dot(down, window, preferred_element_type=jnp.float32).astype(jnp.bfloat16)
                smooth[j, c] = result[:, 0:128]
                smooth[j, c + 1] = result[:, 128:256]
            return carry

        lax.fori_loop(0, 8, smooth_some, 0)

    def pack_chunk(j):
        def pack_some(step, carry):
            c0 = step * 32
            wide = jnp.concatenate(
                [smooth[j, pl.ds(c0, 32), 16 * q:16 * q + 16, :].reshape(512, 128) for q in range(4)], axis=1)
            edges = jnp.dot(wide, pick[...], preferred_element_type=jnp.float32).astype(jnp.bfloat16)
            out_l[j, pl.ds(c0, 32)] = edges[:, 0:128].reshape(32, 16, 128)
            out_r[j, pl.ds(c0, 32)] = edges[:, 128:256].reshape(32, 16, 128)
            return carry

        lax.fori_loop(0, 4, pack_some, 0)

    load.wait()
    for j in ORDER:
        if j == ORDER[2]:
            @pl.when(row > 0)
            def _():
                to_next.wait_recv()

            @pl.when(row < 3)
            def _():
                to_last.wait_recv()

            middle = (row == 1) | (row == 2)
            crossing = (col == 15) | (col == 16)

            @pl.when(middle & (col == 12))
            def _():
                pl.semaphore_signal(go, inc=1, device_id=(row, col + 3), device_id_type=MESH)

            @pl.when(middle & (col == 19))
            def _():
                pl.semaphore_signal(go, inc=1, device_id=(row, col - 3), device_id_type=MESH)

            @pl.when(crossing)
            def _():
                pl.semaphore_wait(go, 1)

            @pl.when(middle & crossing)
            def _():
                pl.semaphore_signal(go, inc=1, device_id=((row - 1) * 3, col), device_id_type=MESH)

            @pl.when(col == 15)
            def _():
                to_right(ORDER[1]).start()

            @pl.when(col == 16)
            def _():
                to_left(ORDER[1]).start()

        smooth_chunk(j)
        if j == ORDER[0]:
            pl.semaphore_wait(barrier, PLANE + GROUP)

            @pl.when(row < 3)
            def _():
                to_next.start()

            @pl.when(row > 0)
            def _():
                to_last.start()

        pack_chunk(j)
        late = j != ORDER[1]

        @pl.when((col < 31) & (late | (col != 15)))
        def _(j=j):
            to_right(j).start()

        @pl.when((col > 0) & (late | (col != 16)))
        def _(j=j):
            to_left(j).start()

    for j in ORDER:
        @pl.when(col > 0)
        def _(j=j):
            to_right(j).wait_recv()

        @pl.when(col < 31)
        def _(j=j):
            to_left(j).wait_recv()

        for h in range(2):
            def coarse_some(step, carry, j=j, h=h):
                c0 = step * 32
                wide = jnp.concatenate(
                    [smooth[j, pl.ds(c0, 32), 32 * h + 16 * k:32 * h + 16 * k + 16, :].reshape(512, 128)
                     for k in range(2)]
                    + [in_l[j, pl.ds(c0, 32)].reshape(512, 128), in_r[j, pl.ds(c0, 32)].reshape(512, 128)], axis=1)
                both = jnp.dot(wide, across[h], preferred_element_type=jnp.float32)
                both = both.astype(jnp.bfloat16).astype(jnp.float32)
                for k in range(2):
                    begin = HW + CHUNK * j + 32 * h + 16 * k
                    value = both[:, 128 * k:128 * k + 128]
                    pixels = skyx[pl.ds(c0, 32), begin:begin + 16, :].reshape(512, 128).astype(jnp.float32)
                    flat_c[pl.ds(2048 * k + c0 * 16, 512), :] = value
                    flat_f[pl.ds(2048 * k + c0 * 16, 512), :] = pixels - value
                return carry

            lax.fori_loop(0, 4, coarse_some, 0)

            def turn_some(k, carry, j=j, h=h):
                for y0 in range(0, 16, 4):
                    for band, flat in ((0, flat_c), (1, flat_f)):
                        lines = []
                        for y in range(y0, y0 + 4):
                            line = flat[pl.ds(2048 * k + y, 128, stride=16), :].astype(jnp.bfloat16)
                            bands_ref[CHUNK * j + 32 * h + 16 * k + y, 128 * band:128 * band + 128, :] = line
                            lines.append(line)
                        wide = jnp.concatenate(lines, axis=1)
                        grams[band] = grams[band] + lax.dot_general(
                            wide, wide, NT, preferred_element_type=jnp.float32)
                return carry

            lax.fori_loop(0, 2, turn_some, 0)

    flag = jnp.where(lax.broadcasted_iota(jnp.int32, (8, 128), 0) == region_ref[0, 0], 1.0, 0.0)
    for q in range(PLANE):
        pieces[q, 0] = grams[0, 8 * q:8 * q + 8, :]
        pieces[q, 1] = grams[1, 8 * q:8 * q + 8, :]
        pieces[q, 2] = flag
    one = []
    for step in range(1, PLANE):
        one.append(pltpu.make_async_remote_copy(
            src_ref=pieces.at[lax.rem(part + step, PLANE)], dst_ref=first.at[step],
            send_sem=s1.at[step], recv_sem=r1.at[step],
            device_id=plane_peer(step), device_id_type=MESH))
    for copy in one:
        copy.start()
    first[0] = pieces[part]
    for copy in one:
        copy.wait_recv()
    for region in range(8):
        total0 = jnp.zeros((8, 128), jnp.float32)
        total1 = jnp.zeros((8, 128), jnp.float32)
        for step in range(PLANE):
            flag = first[step, 2, region:region + 1, :]
            total0 = total0 + flag * first[step, 0]
            total1 = total1 + flag * first[step, 1]
        slots[region, 0] = total0
        slots[region, 1] = total1

    two = []
    for step in range(1, GROUP):
        two.append(pltpu.make_async_remote_copy(
            src_ref=slots, dst_ref=others.at[step],
            send_sem=s2.at[step], recv_sem=r2.at[step],
            device_id=group_peer(step), device_id_type=MESH))
    for copy in two:
        copy.start()
    for copy in two:
        copy.wait_recv()
    sums = []
    for region in range(8):
        pair = []
        for band in range(2):
            total = slots[region, band]
            for step in range(1, GROUP):
                total = total + others[step, region, band]
            pair.append(total)
        sums.append(pair)

    for step in range(PLANE):
        for band in range(2):
            total = jnp.zeros((8, 128), jnp.float32)
            for region in range(8):
                total = total + first[step, 2, region:region + 1, :] * sums[region][band]
            picked[step, band] = total
    three = []
    for step in range(1, PLANE):
        back = lax.rem(part + PLANE - step, PLANE)
        three.append(pltpu.make_async_remote_copy(
            src_ref=picked.at[step], dst_ref=last.at[part],
            send_sem=s3.at[step], recv_sem=r3.at[step],
            device_id=(row, half * PLANE + back), device_id_type=MESH))
    for copy in three:
        copy.start()
    last[part] = picked[0]
    for step in range(1, PLANE):
        ahead = lax.rem(part + step, PLANE)
        pltpu.make_async_remote_copy(
            src_ref=picked.at[step], dst_ref=last.at[ahead],
            send_sem=s3.at[step], recv_sem=r3.at[step],
            device_id=(row, half * PLANE + ahead), device_id_type=MESH).wait_recv()
    for index in range(PLANE):
        for band in range(2):
            gram_ref[band, index * 8:index * 8 + 8, :] = last[index, band]

    @pl.when(row < 3)
    def _():
        to_next.wait_send()

    @pl.when(row > 0)
    def _():
        to_last.wait_send()

    @pl.when(col < 31)
    def _():
        for j in ORDER:
            to_right(j).wait_send()

    @pl.when(col > 0)
    def _():
        for j in ORDER:
            to_left(j).wait_send()

    for copy in one + two + three:
        copy.wait_send()


def front(widths, region, sky):
    bf, f32 = jnp.bfloat16, jnp.float32
    dma = pltpu.SemaphoreType.DMA
    return pl.pallas_call(
        front_kernel,
        out_shape=(pltpu.VMEM((256, 256, 128), bf), pltpu.VMEM((2, 128, 128), f32)),
        in_specs=[pl.BlockSpec(memory_space=pltpu.SMEM)] * 2 + [pl.BlockSpec(memory_space=pl.ANY)],
        out_specs=(pl.BlockSpec(memory_space=pltpu.VMEM), pl.BlockSpec(memory_space=pltpu.VMEM)),
        scratch_shapes=[
            pltpu.VMEM((256, 128), bf),
            pltpu.VMEM((CHANS, 256 + 2 * HW, 128), bf),
            pltpu.VMEM((4, CHANS, CHUNK, 128), bf),
            pltpu.VMEM((4, CHANS, 16, 128), bf),
            pltpu.VMEM((4, CHANS, 16, 128), bf),
            pltpu.VMEM((4, CHANS, 16, 128), bf),
            pltpu.VMEM((4, CHANS, 16, 128), bf),
            pltpu.VMEM((2, 512, 256), bf),
            pltpu.VMEM((512, 256), bf),
            pltpu.VMEM((4096, 128), f32),
            pltpu.VMEM((4096, 128), f32),
            pltpu.VMEM((2, 128, 128), f32),
            pltpu.VMEM((PLANE, 3, 8, 128), f32),
            pltpu.VMEM((PLANE, 3, 8, 128), f32),
            pltpu.VMEM((8, 2, 8, 128), f32),
            pltpu.VMEM((GROUP, 8, 2, 8, 128), f32),
            pltpu.VMEM((PLANE, 2, 8, 128), f32),
            pltpu.VMEM((PLANE, 2, 8, 128), f32),
            pltpu.SemaphoreType.REGULAR,
            dma, dma((2,)), dma((2,)), dma((2, 4)), dma((2, 4)),
            dma((PLANE,)), dma((PLANE,)), dma((GROUP,)), dma((GROUP,)), dma((PLANE,)), dma((PLANE,)),
        ],
        compiler_params=pltpu.CompilerParams(
            collective_id=1, has_side_effects=True, vmem_limit_bytes=40 * 1024 * 1024),
        name="front",
    )(widths, region, sky)


def weights_of(grams, priors, cheb_t, keep):
    lanes = lax.broadcasted_iota(jnp.int32, (8, 128), 1)
    subs = lax.broadcasted_iota(jnp.int32, (8, 128), 0)
    mats = []
    for band in range(2):
        blocks = []
        for i in range(16):
            block = grams[band][i * 8:i * 8 + 8, :]
            diag = jnp.where(lanes == subs + 8 * i, priors[band], 0.0)
            blocks.append(block / 524288.0 + diag)
        blocks.append(cheb_t)
        mats.append(blocks)
    for k in range(128):
        at, off = k // 8, k % 8
        hit = lanes[0:1, :] == k
        for band in range(2):
            m = mats[band]
            cols = [jnp.broadcast_to(b[:, k:k + 1], (8, 128)) for b in m]
            inv = 1.0 / cols[at][off:off + 1, :]
            line = m[at][off:off + 1, :] * inv
            line = jnp.where(hit, 1.0 - inv, line)
            mats[band] = [b - c * line for b, c in zip(m, cols)]
    out = []
    for band in range(2):
        mixed = mats[band][16] * keep
        kept = cheb_t * keep
        small = lax.dot_general(kept, mixed, (((1,), (1,)), ((), ())), precision=HIGH,
                                preferred_element_type=jnp.float32)
        eye = (lax.broadcasted_iota(jnp.int32, (8, 8), 0) == lax.broadcasted_iota(jnp.int32, (8, 8), 1))
        small = small + jnp.where(eye, 1.0 - keep[:, 0:8], 0.0)
        out.append((small, mixed))
    weights = []
    for small, mixed in out:
        for k in range(8):
            fac = small[:, k:k + 1]
            inv = 1.0 / fac[k:k + 1, :]
            shift = jnp.where(subs[:, 0:1] == k, 1.0, 0.0)
            fac = fac - shift
            srow = small[k:k + 1, :] * inv
            mrow = mixed[k:k + 1, :] * inv
            small = small - fac * srow
            mixed = mixed - fac * mrow
        weights.append(mixed)
    return weights


def chebyshev_rows():
    lane = lax.broadcasted_iota(jnp.int32, (8, 128), 1).astype(jnp.float32)
    order = lax.broadcasted_iota(jnp.int32, (8, 128), 0)
    position = (2.0 * lane + 1.0) / CHANS - 1.0
    terms = [jnp.ones_like(position), position]
    rows = jnp.where(order == 0, terms[0], position)
    for m in range(2, MMAX):
        terms.append(2.0 * position * terms[-1] - terms[-2])
        rows = jnp.where(order == m, terms[-1], rows)
    return rows


def back_kernel(region_ref, rank_ref, gram_ref, prior_ref, bands_ref, out_ref, proj, flat, ready, sems):
    cheb_t = chebyshev_rows()
    rank = rank_ref[region_ref[0, 0]]
    keep = jnp.where(lax.broadcasted_iota(jnp.int32, (8, 128), 0) < rank, 1.0, 0.0)
    weights = weights_of([gram_ref[0], gram_ref[1]], [prior_ref[0:1, :], prior_ref[1:2, :]], cheb_t, keep)
    kept = cheb_t * keep
    for band in range(2):
        part = lax.dot_general(kept, weights[band], (((0,), (0,)), ((), ())), precision=HIGH,
                               preferred_element_type=jnp.float32)
        proj[:, 128 * band:128 * band + 128] = part.astype(jnp.bfloat16)

    def put(slot, base):
        return pltpu.make_async_copy(ready.at[slot], out_ref.at[:, pl.ds(base, 16), :], sems.at[slot])

    def block(step, carry):
        for slot in range(2):
            base = pl.multiple_of(step * 32 + slot * 16, 16)
            for y in range(0, 16, 2):
                pair = jnp.concatenate([bands_ref[base + y], bands_ref[base + y + 1]], axis=1)
                removed = jnp.dot(proj[...], pair, preferred_element_type=jnp.float32)
                wide = pair.astype(jnp.float32)
                result = wide[0:128] + wide[128:256] - removed
                flat[pl.ds(2048 * slot + y, 128, stride=16), :] = result[:, 0:128]
                flat[pl.ds(2048 * slot + y + 1, 128, stride=16), :] = result[:, 128:256]

            @pl.when(step > 0)
            def _(slot=slot):
                put(slot, 0).wait()

            ready[slot] = flat[2048 * slot:2048 * slot + 2048, :].reshape(128, 16, 128).astype(jnp.bfloat16)
            put(slot, base).start()
        return carry

    lax.fori_loop(0, 8, block, 0)
    put(0, 0).wait()
    put(1, 0).wait()


def back(region, ranks, grams, prior_var, bands):
    whole = pl.BlockSpec(memory_space=pltpu.VMEM)
    bands = pltpu.with_memory_space_constraint(bands, pltpu.VMEM)
    return pl.pallas_call(
        back_kernel,
        out_shape=jax.ShapeDtypeStruct((128, 256, 128), jnp.bfloat16),
        in_specs=[pl.BlockSpec(memory_space=pltpu.SMEM)] * 2 + [whole] * 3,
        out_specs=pl.BlockSpec(memory_space=pl.ANY),
        scratch_shapes=[pltpu.VMEM((128, 256), jnp.bfloat16), pltpu.VMEM((4096, 128), jnp.float32),
                        pltpu.VMEM((2, 128, 16, 128), jnp.bfloat16), pltpu.SemaphoreType.DMA((2,))],
        compiler_params=pltpu.CompilerParams(vmem_limit_bytes=16 * 1024 * 1024),
        name="back",
    )(region, ranks, grams, prior_var, bands)


def local(sky, kernel_widths, prior_var, tile_region, region_rank):
    bands, own_gram = front(kernel_widths, tile_region, sky)
    return back(tile_region, region_rank, own_gram, prior_var, bands)


def solution(mesh):
    return jax.shard_map(
        local,
        mesh=mesh,
        in_specs=(P(None, "row", "col"), P(), P(), P("row", "col"), P()),
        out_specs=P(None, "row", "col"),
        check_vma=False,
    )
```

```python
import math
import jax
import jax.numpy as jnp
from jax import lax
from jax.experimental import pallas as pl
from jax.experimental.pallas import tpu as pltpu
from jax.sharding import PartitionSpec as P

HW = 32
MMAX = 8
TPR = 16
PLANE = 16
GROUP = 8
CHANS = 128
CHUNK = 64
MESH = pl.DeviceIdType.MESH
HIGH = lax.Precision.HIGHEST
NT = (((1,), (1,)), ((), ()))


def taps_table(down_width, across_width):
    line = lax.broadcasted_iota(jnp.int32, (256, 128), 0)
    lane = lax.broadcasted_iota(jnp.int32, (256, 128), 1)
    first = line < 192
    offsets = jnp.where(first, line - lane - HW, lane - (line - 192) - HW).astype(jnp.float32)
    spread = jnp.where(first, across_width, down_width).astype(jnp.float32)
    values = (1.0 + jnp.cos(math.pi * offsets / (spread + 1.0))) / (2.0 * spread + 2.0)
    return jnp.where(jnp.abs(offsets) <= spread, values, 0.0).astype(jnp.bfloat16)


def front_kernel(widths_ref, region_ref, sky_ref, bands_ref, gram_ref,
                 table_ref, skyx, smooth, out_l, out_r, in_l, in_r, across, pick, flat_c, flat_f, grams, pieces,
                 first, slots, others, picked, last,
                 sky_sem, ys, yr, xs, xr, s1, r1, s2, r2, s3, r3):
    row = lax.axis_index("row")
    col = lax.axis_index("col")
    part = lax.rem(col, PLANE)
    half = lax.div(col, PLANE)
    place = half * 4 + row

    def plane_peer(step):
        return (row, half * PLANE + lax.rem(part + step, PLANE))

    def group_peer(step):
        other = lax.rem(place + step, GROUP)
        return (lax.rem(other, 4), lax.div(other, 4) * PLANE + part)

    barrier = pltpu.get_barrier_semaphore()
    for step in (1, 31):
        pl.semaphore_signal(barrier, inc=1, device_id=(row, lax.rem(col + step, 32)), device_id_type=MESH)
    for step in range(1, GROUP):
        pl.semaphore_signal(barrier, inc=1, device_id=group_peer(step), device_id_type=MESH)
    for step in range(1, PLANE):
        pl.semaphore_signal(barrier, inc=1, device_id=plane_peer(step), device_id_type=MESH)

    load = pltpu.make_async_copy(sky_ref, skyx.at[:, HW:HW + 256, :], sky_sem)
    load.start()

    table_ref[...] = taps_table(widths_ref[0], widths_ref[1])

    zero = jnp.zeros((512, 256), jnp.bfloat16)
    own = table_ref[HW:HW + 128, :]
    for h in range(2):
        across[h] = zero
        across[h, 0:128, 0:128] = own
        across[h, 128:256, 128:256] = own
        for k in range(2):
            base = HW * (2 * h + k)
            across[h, 256 + base:256 + base + HW, 128 * k:128 * k + 128] = table_ref[0:HW, :]
            across[h, 384 + base:384 + base + HW, 128 * k:128 * k + 128] = table_ref[160:192, :]
    source = lax.broadcasted_iota(jnp.int32, (512, 256), 0)
    target = lax.broadcasted_iota(jnp.int32, (512, 256), 1)
    lane = target % 128
    wanted = (lane // HW) * 128 + lane % HW + jnp.where(target >= 128, 96, 0)
    pick[...] = jnp.where(source == wanted, 1.0, 0.0).astype(jnp.bfloat16)
    down = table_ref[192:256, :]
    grams[...] = jnp.zeros((2, 128, 128), jnp.float32)

    @pl.when(row == 0)
    def _():
        skyx[:, 0:HW, :] = jnp.zeros((CHANS, HW, 128), jnp.bfloat16)

    @pl.when(row == 3)
    def _():
        skyx[:, HW + 256:, :] = jnp.zeros((CHANS, HW, 128), jnp.bfloat16)

    @pl.when(col == 0)
    def _():
        in_l[...] = jnp.zeros(in_l.shape, jnp.bfloat16)

    @pl.when(col == 31)
    def _():
        in_r[...] = jnp.zeros(in_r.shape, jnp.bfloat16)

    to_next = pltpu.make_async_remote_copy(
        src_ref=sky_ref.at[:, 256 - HW:256, :], dst_ref=skyx.at[:, 0:HW, :],
        send_sem=ys.at[0], recv_sem=yr.at[0], device_id=(lax.rem(row + 1, 4), col), device_id_type=MESH)
    to_last = pltpu.make_async_remote_copy(
        src_ref=sky_ref.at[:, 0:HW, :], dst_ref=skyx.at[:, HW + 256:, :],
        send_sem=ys.at[1], recv_sem=yr.at[1], device_id=(lax.rem(row + 3, 4), col), device_id_type=MESH)

    def to_right(j):
        return pltpu.make_async_remote_copy(
            src_ref=out_r.at[j], dst_ref=in_l.at[j], send_sem=xs.at[0, j], recv_sem=xr.at[0, j],
            device_id=(row, lax.rem(col + 1, 32)), device_id_type=MESH)

    def to_left(j):
        return pltpu.make_async_remote_copy(
            src_ref=out_l.at[j], dst_ref=in_r.at[j], send_sem=xs.at[1, j], recv_sem=xr.at[1, j],
            device_id=(row, lax.rem(col + 31, 32)), device_id_type=MESH)

    def smooth_chunk(j):
        start = pl.multiple_of(CHUNK * j, CHUNK)

        def smooth_some(step, carry):
            c0 = step * 16
            for p in range(8):
                c = c0 + 2 * p
                window = jnp.concatenate(
                    [skyx[c, pl.ds(start, 128), :], skyx[c + 1, pl.ds(start, 128), :]], axis=1)
                result = jnp.dot(down, window, preferred_element_type=jnp.float32).astype(jnp.bfloat16)
                smooth[j, c] = result[:, 0:128]
                smooth[j, c + 1] = result[:, 128:256]
            return carry

        lax.fori_loop(0, 8, smooth_some, 0)

    def pack_chunk(j):
        def pack_some(step, carry):
            c0 = step * 32
            wide = jnp.concatenate(
                [smooth[j, pl.ds(c0, 32), 16 * q:16 * q + 16, :].reshape(512, 128) for q in range(4)], axis=1)
            edges = jnp.dot(wide, pick[...], preferred_element_type=jnp.float32).astype(jnp.bfloat16)
            out_l[j, pl.ds(c0, 32)] = edges[:, 0:128].reshape(32, 16, 128)
            out_r[j, pl.ds(c0, 32)] = edges[:, 128:256].reshape(32, 16, 128)
            return carry

        lax.fori_loop(0, 4, pack_some, 0)

    load.wait()
    order = (1, 2, jnp.where(row == 2, 3, 0), jnp.where(row == 2, 0, 3))
    for turn, j in enumerate(order):
        if turn == 2:
            @pl.when((row == 1) | (row == 3))
            def _():
                to_next.wait_recv()

            @pl.when(row == 2)
            def _():
                to_last.wait_recv()

        if turn == 3:
            @pl.when((row == 0) | (row == 1))
            def _():
                to_last.wait_recv()

            @pl.when(row == 2)
            def _():
                to_next.wait_recv()

        smooth_chunk(j)
        if turn == 0:
            pl.semaphore_wait(barrier, PLANE + GROUP)

            @pl.when(row < 3)
            def _():
                to_next.start()

            @pl.when(row > 0)
            def _():
                to_last.start()

        pack_chunk(j)

        @pl.when(col < 31)
        def _(j=j):
            to_right(j).start()

        @pl.when(col > 0)
        def _(j=j):
            to_left(j).start()

    for j in order:
        @pl.when(col > 0)
        def _(j=j):
            to_right(j).wait_recv()

        @pl.when(col < 31)
        def _(j=j):
            to_left(j).wait_recv()

        for h in range(2):
            def coarse_some(step, carry, j=j, h=h):
                c0 = step * 32
                wide = jnp.concatenate(
                    [smooth[j, pl.ds(c0, 32), 32 * h + 16 * k:32 * h + 16 * k + 16, :].reshape(512, 128)
                     for k in range(2)]
                    + [in_l[j, pl.ds(c0, 32)].reshape(512, 128), in_r[j, pl.ds(c0, 32)].reshape(512, 128)], axis=1)
                both = jnp.dot(wide, across[h], preferred_element_type=jnp.float32)
                both = both.astype(jnp.bfloat16).astype(jnp.float32)
                for k in range(2):
                    begin = pl.multiple_of(HW + CHUNK * j + 32 * h + 16 * k, 16)
                    value = both[:, 128 * k:128 * k + 128]
                    pixels = skyx[pl.ds(c0, 32), pl.ds(begin, 16), :].reshape(512, 128).astype(jnp.float32)
                    flat_c[pl.ds(2048 * k + c0 * 16, 512), :] = value
                    flat_f[pl.ds(2048 * k + c0 * 16, 512), :] = pixels - value
                return carry

            lax.fori_loop(0, 4, coarse_some, 0)

            def turn_some(k, carry, j=j, h=h):
                for y0 in range(0, 16, 4):
                    for band, flat in ((0, flat_c), (1, flat_f)):
                        lines = []
                        for y in range(y0, y0 + 4):
                            line = flat[pl.ds(2048 * k + y, 128, stride=16), :].astype(jnp.bfloat16)
                            bands_ref[CHUNK * j + 32 * h + 16 * k + y, 128 * band:128 * band + 128, :] = line
                            lines.append(line)
                        wide = jnp.concatenate(lines, axis=1)
                        grams[band] = grams[band] + lax.dot_general(
                            wide, wide, NT, preferred_element_type=jnp.float32)
                return carry

            lax.fori_loop(0, 2, turn_some, 0)

    flag = jnp.where(lax.broadcasted_iota(jnp.int32, (8, 128), 0) == region_ref[0, 0], 1.0, 0.0)
    for q in range(PLANE):
        pieces[q, 0] = grams[0, 8 * q:8 * q + 8, :]
        pieces[q, 1] = grams[1, 8 * q:8 * q + 8, :]
        pieces[q, 2] = flag
    one = []
    for step in range(1, PLANE):
        one.append(pltpu.make_async_remote_copy(
            src_ref=pieces.at[lax.rem(part + step, PLANE)], dst_ref=first.at[step],
            send_sem=s1.at[step], recv_sem=r1.at[step],
            device_id=plane_peer(step), device_id_type=MESH))
    for copy in one:
        copy.start()
    first[0] = pieces[part]
    for copy in one:
        copy.wait_recv()
    for region in range(8):
        total0 = jnp.zeros((8, 128), jnp.float32)
        total1 = jnp.zeros((8, 128), jnp.float32)
        for step in range(PLANE):
            flag = first[step, 2, region:region + 1, :]
            total0 = total0 + flag * first[step, 0]
            total1 = total1 + flag * first[step, 1]
        slots[region, 0] = total0
        slots[region, 1] = total1

    two = []
    for step in range(1, GROUP):
        two.append(pltpu.make_async_remote_copy(
            src_ref=slots, dst_ref=others.at[step],
            send_sem=s2.at[step], recv_sem=r2.at[step],
            device_id=group_peer(step), device_id_type=MESH))
    for copy in two:
        copy.start()
    for copy in two:
        copy.wait_recv()
    sums = []
    for region in range(8):
        pair = []
        for band in range(2):
            total = slots[region, band]
            for step in range(1, GROUP):
                total = total + others[step, region, band]
            pair.append(total)
        sums.append(pair)

    for step in range(PLANE):
        for band in range(2):
            total = jnp.zeros((8, 128), jnp.float32)
            for region in range(8):
                total = total + first[step, 2, region:region + 1, :] * sums[region][band]
            picked[step, band] = total
    three = []
    for step in range(1, PLANE):
        back = lax.rem(part + PLANE - step, PLANE)
        three.append(pltpu.make_async_remote_copy(
            src_ref=picked.at[step], dst_ref=last.at[part],
            send_sem=s3.at[step], recv_sem=r3.at[step],
            device_id=(row, half * PLANE + back), device_id_type=MESH))
    for copy in three:
        copy.start()
    last[part] = picked[0]
    for step in range(1, PLANE):
        ahead = lax.rem(part + step, PLANE)
        pltpu.make_async_remote_copy(
            src_ref=picked.at[step], dst_ref=last.at[ahead],
            send_sem=s3.at[step], recv_sem=r3.at[step],
            device_id=(row, half * PLANE + ahead), device_id_type=MESH).wait_recv()
    for index in range(PLANE):
        for band in range(2):
            gram_ref[band, index * 8:index * 8 + 8, :] = last[index, band]

    @pl.when(row < 3)
    def _():
        to_next.wait_send()

    @pl.when(row > 0)
    def _():
        to_last.wait_send()

    @pl.when(col < 31)
    def _():
        for j in range(4):
            to_right(j).wait_send()

    @pl.when(col > 0)
    def _():
        for j in range(4):
            to_left(j).wait_send()

    for copy in one + two + three:
        copy.wait_send()


def front(widths, region, sky):
    bf, f32 = jnp.bfloat16, jnp.float32
    dma = pltpu.SemaphoreType.DMA
    return pl.pallas_call(
        front_kernel,
        out_shape=(pltpu.VMEM((256, 256, 128), bf), pltpu.VMEM((2, 128, 128), f32)),
        in_specs=[pl.BlockSpec(memory_space=pltpu.SMEM)] * 2 + [pl.BlockSpec(memory_space=pl.ANY)],
        out_specs=(pl.BlockSpec(memory_space=pltpu.VMEM), pl.BlockSpec(memory_space=pltpu.VMEM)),
        scratch_shapes=[
            pltpu.VMEM((256, 128), bf),
            pltpu.VMEM((CHANS, 256 + 2 * HW, 128), bf),
            pltpu.VMEM((4, CHANS, CHUNK, 128), bf),
            pltpu.VMEM((4, CHANS, 16, 128), bf),
            pltpu.VMEM((4, CHANS, 16, 128), bf),
            pltpu.VMEM((4, CHANS, 16, 128), bf),
            pltpu.VMEM((4, CHANS, 16, 128), bf),
            pltpu.VMEM((2, 512, 256), bf),
            pltpu.VMEM((512, 256), bf),
            pltpu.VMEM((4096, 128), f32),
            pltpu.VMEM((4096, 128), f32),
            pltpu.VMEM((2, 128, 128), f32),
            pltpu.VMEM((PLANE, 3, 8, 128), f32),
            pltpu.VMEM((PLANE, 3, 8, 128), f32),
            pltpu.VMEM((8, 2, 8, 128), f32),
            pltpu.VMEM((GROUP, 8, 2, 8, 128), f32),
            pltpu.VMEM((PLANE, 2, 8, 128), f32),
            pltpu.VMEM((PLANE, 2, 8, 128), f32),
            dma, dma((2,)), dma((2,)), dma((2, 4)), dma((2, 4)),
            dma((PLANE,)), dma((PLANE,)), dma((GROUP,)), dma((GROUP,)), dma((PLANE,)), dma((PLANE,)),
        ],
        compiler_params=pltpu.CompilerParams(
            collective_id=1, has_side_effects=True, vmem_limit_bytes=40 * 1024 * 1024),
        name="front",
    )(widths, region, sky)


WIDE = 4


def weights_of(grams, priors, cheb_t, keep):
    lanes = lax.broadcasted_iota(jnp.int32, (8, 128), 1)
    subs = lax.broadcasted_iota(jnp.int32, (8, 128), 0)
    mats = []
    for band in range(2):
        blocks = []
        for i in range(16):
            block = grams[band][i * 8:i * 8 + 8, :]
            diag = jnp.where(lanes == subs + 8 * i, priors[band], 0.0)
            blocks.append(block / 524288.0 + diag)
        blocks.append(cheb_t)
        mats.append(blocks)
    for k in range(0, 128, WIDE):
        at, off = k // 8, k % 8
        for band in range(2):
            m = mats[band]
            cols = [[jnp.broadcast_to(b[:, k + p:k + p + 1], (8, 128)) for b in m] for p in range(WIDE)]
            hit = (lanes >= k) & (lanes < k + WIDE)
            rows = [jnp.where(hit[0:1], jnp.where(lanes[0:1] == k + i, -1.0, 0.0), m[at][off + i:off + i + 1, :])
                    for i in range(WIDE)]
            d = [[cols[p][at][off + i:off + i + 1, :] for p in range(WIDE)] for i in range(WIDE)]
            inv = []
            for i in range(WIDE):
                inv.append(1.0 / d[i][i])
                for l in range(i + 1, WIDE):
                    t = d[l][i] * inv[i]
                    rows[l] = rows[l] - t * rows[i]
                    for j in range(i + 1, WIDE):
                        d[l][j] = d[l][j] - t * d[i][j]
            for i in reversed(range(WIDE)):
                line = rows[i]
                for j in range(i + 1, WIDE):
                    line = line - d[i][j] * rows[j]
                rows[i] = line * inv[i]
            fresh = []
            for index, b in enumerate(m):
                b = jnp.where(hit, 0.0, b)
                for p in range(WIDE):
                    b = b - cols[p][index] * rows[p]
                fresh.append(b)
            mats[band] = fresh
    out = []
    for band in range(2):
        mixed = mats[band][16] * keep
        kept = cheb_t * keep
        small = lax.dot_general(kept, mixed, (((1,), (1,)), ((), ())), precision=HIGH,
                                preferred_element_type=jnp.float32)
        eye = (lax.broadcasted_iota(jnp.int32, (8, 8), 0) == lax.broadcasted_iota(jnp.int32, (8, 8), 1))
        small = small + jnp.where(eye, 1.0 - keep[:, 0:8], 0.0)
        out.append((small, mixed))
    weights = []
    for small, mixed in out:
        for k in range(8):
            fac = small[:, k:k + 1]
            inv = 1.0 / fac[k:k + 1, :]
            shift = jnp.where(subs[:, 0:1] == k, 1.0, 0.0)
            fac = fac - shift
            srow = small[k:k + 1, :] * inv
            mrow = mixed[k:k + 1, :] * inv
            small = small - fac * srow
            mixed = mixed - fac * mrow
        weights.append(mixed)
    return weights


def chebyshev_rows():
    lane = lax.broadcasted_iota(jnp.int32, (8, 128), 1).astype(jnp.float32)
    order = lax.broadcasted_iota(jnp.int32, (8, 128), 0)
    position = (2.0 * lane + 1.0) / CHANS - 1.0
    terms = [jnp.ones_like(position), position]
    rows = jnp.where(order == 0, terms[0], position)
    for m in range(2, MMAX):
        terms.append(2.0 * position * terms[-1] - terms[-2])
        rows = jnp.where(order == m, terms[-1], rows)
    return rows


def back_kernel(region_ref, rank_ref, gram_ref, prior_ref, bands_ref, out_ref, proj, flat, ready, sems):
    cheb_t = chebyshev_rows()
    rank = rank_ref[region_ref[0, 0]]
    keep = jnp.where(lax.broadcasted_iota(jnp.int32, (8, 128), 0) < rank, 1.0, 0.0)
    weights = weights_of([gram_ref[0], gram_ref[1]], [prior_ref[0:1, :], prior_ref[1:2, :]], cheb_t, keep)
    kept = cheb_t * keep
    for band in range(2):
        part = lax.dot_general(kept, weights[band], (((0,), (0,)), ((), ())), precision=HIGH,
                               preferred_element_type=jnp.float32)
        proj[:, 128 * band:128 * band + 128] = part.astype(jnp.bfloat16)

    def put(slot, base):
        return pltpu.make_async_copy(ready.at[slot], out_ref.at[:, pl.ds(base, 16), :], sems.at[slot])

    def block(step, carry):
        for slot in range(2):
            base = pl.multiple_of(step * 32 + slot * 16, 16)
            for y in range(0, 16, 2):
                pair = jnp.concatenate([bands_ref[base + y], bands_ref[base + y + 1]], axis=1)
                removed = jnp.dot(proj[...], pair, preferred_element_type=jnp.float32)
                wide = pair.astype(jnp.float32)
                result = wide[0:128] + wide[128:256] - removed
                flat[pl.ds(2048 * slot + y, 128, stride=16), :] = result[:, 0:128]
                flat[pl.ds(2048 * slot + y + 1, 128, stride=16), :] = result[:, 128:256]

            @pl.when(step > 0)
            def _(slot=slot):
                put(slot, 0).wait()

            ready[slot] = flat[2048 * slot:2048 * slot + 2048, :].reshape(128, 16, 128).astype(jnp.bfloat16)
            put(slot, base).start()
        return carry

    lax.fori_loop(0, 8, block, 0)
    put(0, 0).wait()
    put(1, 0).wait()


def back(region, ranks, grams, prior_var, bands):
    whole = pl.BlockSpec(memory_space=pltpu.VMEM)
    bands = pltpu.with_memory_space_constraint(bands, pltpu.VMEM)
    return pl.pallas_call(
        back_kernel,
        out_shape=jax.ShapeDtypeStruct((128, 256, 128), jnp.bfloat16),
        in_specs=[pl.BlockSpec(memory_space=pltpu.SMEM)] * 2 + [whole] * 3,
        out_specs=pl.BlockSpec(memory_space=pl.ANY),
        scratch_shapes=[pltpu.VMEM((128, 256), jnp.bfloat16), pltpu.VMEM((4096, 128), jnp.float32),
                        pltpu.VMEM((2, 128, 16, 128), jnp.bfloat16), pltpu.SemaphoreType.DMA((2,))],
        compiler_params=pltpu.CompilerParams(vmem_limit_bytes=16 * 1024 * 1024),
        name="back",
    )(region, ranks, grams, prior_var, bands)


def local(sky, kernel_widths, prior_var, tile_region, region_rank):
    bands, own_gram = front(kernel_widths, tile_region, sky)
    return back(tile_region, region_rank, own_gram, prior_var, bands)


def solution(mesh):
    return jax.shard_map(
        local,
        mesh=mesh,
        in_specs=(P(None, "row", "col"), P(), P(), P("row", "col"), P()),
        out_specs=P(None, "row", "col"),
        check_vma=False,
    )
```

```python
import math
import jax
import jax.numpy as jnp
from jax import lax
from jax.experimental import pallas as pl
from jax.experimental.pallas import tpu as pltpu
from jax.sharding import PartitionSpec as P

HW = 32
MMAX = 8
TPR = 16
PLANE = 16
GROUP = 8
CHANS = 128
CHUNK = 64
MESH = pl.DeviceIdType.MESH
HIGH = lax.Precision.HIGHEST
NT = (((1,), (1,)), ((), ()))


def taps_table(down_width, across_width):
    line = lax.broadcasted_iota(jnp.int32, (256, 128), 0)
    lane = lax.broadcasted_iota(jnp.int32, (256, 128), 1)
    first = line < 192
    offsets = jnp.where(first, line - lane - HW, lane - (line - 192) - HW).astype(jnp.float32)
    spread = jnp.where(first, across_width, down_width).astype(jnp.float32)
    values = (1.0 + jnp.cos(math.pi * offsets / (spread + 1.0))) / (2.0 * spread + 2.0)
    return jnp.where(jnp.abs(offsets) <= spread, values, 0.0).astype(jnp.bfloat16)


def front_kernel(widths_ref, region_ref, sky_ref, bands_ref, gram_ref,
                 table_ref, skyx, smooth, out_l, out_r, in_l, in_r, across, pick, flat_c, flat_f, grams, pieces,
                 first, slots, others, picked, last,
                 go, sky_sem, ys, yr, xs, xr, s1, r1, s2, r2, s3, r3):
    row = lax.axis_index("row")
    col = lax.axis_index("col")
    part = lax.rem(col, PLANE)
    half = lax.div(col, PLANE)
    place = half * 4 + row

    def plane_peer(step):
        return (row, half * PLANE + lax.rem(part + step, PLANE))

    def group_peer(step):
        other = lax.rem(place + step, GROUP)
        return (lax.rem(other, 4), lax.div(other, 4) * PLANE + part)

    barrier = pltpu.get_barrier_semaphore()
    for step in (1, 31):
        pl.semaphore_signal(barrier, inc=1, device_id=(row, lax.rem(col + step, 32)), device_id_type=MESH)
    for step in range(1, GROUP):
        pl.semaphore_signal(barrier, inc=1, device_id=group_peer(step), device_id_type=MESH)
    for step in range(1, PLANE):
        pl.semaphore_signal(barrier, inc=1, device_id=plane_peer(step), device_id_type=MESH)

    load = pltpu.make_async_copy(sky_ref, skyx.at[:, HW:HW + 256, :], sky_sem)
    load.start()

    table_ref[...] = taps_table(widths_ref[0], widths_ref[1])

    zero = jnp.zeros((512, 256), jnp.bfloat16)
    own = table_ref[HW:HW + 128, :]
    for h in range(2):
        across[h] = zero
        across[h, 0:128, 0:128] = own
        across[h, 128:256, 128:256] = own
        for k in range(2):
            base = HW * (2 * h + k)
            across[h, 256 + base:256 + base + HW, 128 * k:128 * k + 128] = table_ref[0:HW, :]
            across[h, 384 + base:384 + base + HW, 128 * k:128 * k + 128] = table_ref[160:192, :]
    source = lax.broadcasted_iota(jnp.int32, (512, 256), 0)
    target = lax.broadcasted_iota(jnp.int32, (512, 256), 1)
    lane = target % 128
    wanted = (lane // HW) * 128 + lane % HW + jnp.where(target >= 128, 96, 0)
    pick[...] = jnp.where(source == wanted, 1.0, 0.0).astype(jnp.bfloat16)
    down = table_ref[192:256, :]
    grams[...] = jnp.zeros((2, 128, 128), jnp.float32)

    @pl.when(row == 0)
    def _():
        skyx[:, 0:HW, :] = jnp.zeros((CHANS, HW, 128), jnp.bfloat16)

    @pl.when(row == 3)
    def _():
        skyx[:, HW + 256:, :] = jnp.zeros((CHANS, HW, 128), jnp.bfloat16)

    @pl.when(col == 0)
    def _():
        in_l[...] = jnp.zeros(in_l.shape, jnp.bfloat16)

    @pl.when(col == 31)
    def _():
        in_r[...] = jnp.zeros(in_r.shape, jnp.bfloat16)

    to_next = pltpu.make_async_remote_copy(
        src_ref=sky_ref.at[:, 256 - HW:256, :], dst_ref=skyx.at[:, 0:HW, :],
        send_sem=ys.at[0], recv_sem=yr.at[0], device_id=(lax.rem(row + 1, 4), col), device_id_type=MESH)
    to_last = pltpu.make_async_remote_copy(
        src_ref=sky_ref.at[:, 0:HW, :], dst_ref=skyx.at[:, HW + 256:, :],
        send_sem=ys.at[1], recv_sem=yr.at[1], device_id=(lax.rem(row + 3, 4), col), device_id_type=MESH)

    def to_right(j):
        return pltpu.make_async_remote_copy(
            src_ref=out_r.at[j], dst_ref=in_l.at[j], send_sem=xs.at[0, j], recv_sem=xr.at[0, j],
            device_id=(row, lax.rem(col + 1, 32)), device_id_type=MESH)

    def to_left(j):
        return pltpu.make_async_remote_copy(
            src_ref=out_l.at[j], dst_ref=in_r.at[j], send_sem=xs.at[1, j], recv_sem=xr.at[1, j],
            device_id=(row, lax.rem(col + 31, 32)), device_id_type=MESH)

    def smooth_chunk(j):
        start = pl.multiple_of(CHUNK * j, CHUNK)

        def smooth_some(step, carry):
            c0 = step * 16
            for p in range(8):
                c = c0 + 2 * p
                window = jnp.concatenate(
                    [skyx[c, pl.ds(start, 128), :], skyx[c + 1, pl.ds(start, 128), :]], axis=1)
                result = jnp.dot(down, window, preferred_element_type=jnp.float32).astype(jnp.bfloat16)
                smooth[j, c] = result[:, 0:128]
                smooth[j, c + 1] = result[:, 128:256]
            return carry

        lax.fori_loop(0, 8, smooth_some, 0)

    def pack_chunk(j):
        def pack_some(step, carry):
            c0 = step * 32
            wide = jnp.concatenate(
                [smooth[j, pl.ds(c0, 32), 16 * q:16 * q + 16, :].reshape(512, 128) for q in range(4)], axis=1)
            edges = jnp.dot(wide, pick[...], preferred_element_type=jnp.float32).astype(jnp.bfloat16)
            out_l[j, pl.ds(c0, 32)] = edges[:, 0:128].reshape(32, 16, 128)
            out_r[j, pl.ds(c0, 32)] = edges[:, 128:256].reshape(32, 16, 128)
            return carry

        lax.fori_loop(0, 4, pack_some, 0)

    load.wait()
    middle = (row == 1) | (row == 2)
    crossing = (col == 15) | (col == 16)
    order = (1, 2, jnp.where(row == 2, 3, 0), jnp.where(row == 2, 0, 3))
    for turn, j in enumerate(order):
        if turn == 2:
            @pl.when((row == 1) | (row == 3))
            def _():
                to_next.wait_recv()

            @pl.when(row == 2)
            def _():
                to_last.wait_recv()

        if turn == 3:
            @pl.when((row == 0) | (row == 1))
            def _():
                to_last.wait_recv()

            @pl.when(row == 2)
            def _():
                to_next.wait_recv()

            @pl.when(middle & (col == 12))
            def _():
                pl.semaphore_signal(go, inc=1, device_id=(row, col + 3), device_id_type=MESH)

            @pl.when(middle & (col == 19))
            def _():
                pl.semaphore_signal(go, inc=1, device_id=(row, col - 3), device_id_type=MESH)

        smooth_chunk(j)
        if turn == 0:
            pl.semaphore_wait(barrier, PLANE + GROUP)

            @pl.when(row < 3)
            def _():
                to_next.start()

            @pl.when(row > 0)
            def _():
                to_last.start()

        pack_chunk(j)

        @pl.when((col < 31) & (col != 15))
        def _(j=j):
            to_right(j).start()

        @pl.when((col > 0) & (col != 16))
        def _(j=j):
            to_left(j).start()

    @pl.when(crossing)
    def _():
        pl.semaphore_wait(go, 1)

    @pl.when(middle & crossing)
    def _():
        pl.semaphore_signal(go, inc=1, device_id=((row - 1) * 3, col), device_id_type=MESH)

    @pl.when(col == 15)
    def _():
        for j in order:
            to_right(j).start()

    @pl.when(col == 16)
    def _():
        for j in order:
            to_left(j).start()

    for j in order:
        @pl.when(col > 0)
        def _(j=j):
            to_right(j).wait_recv()

        @pl.when(col < 31)
        def _(j=j):
            to_left(j).wait_recv()

        for h in range(2):
            def coarse_some(step, carry, j=j, h=h):
                c0 = step * 32
                wide = jnp.concatenate(
                    [smooth[j, pl.ds(c0, 32), 32 * h + 16 * k:32 * h + 16 * k + 16, :].reshape(512, 128)
                     for k in range(2)]
                    + [in_l[j, pl.ds(c0, 32)].reshape(512, 128), in_r[j, pl.ds(c0, 32)].reshape(512, 128)], axis=1)
                both = jnp.dot(wide, across[h], preferred_element_type=jnp.float32)
                both = both.astype(jnp.bfloat16).astype(jnp.float32)
                for k in range(2):
                    begin = pl.multiple_of(HW + CHUNK * j + 32 * h + 16 * k, 16)
                    value = both[:, 128 * k:128 * k + 128]
                    pixels = skyx[pl.ds(c0, 32), pl.ds(begin, 16), :].reshape(512, 128).astype(jnp.float32)
                    flat_c[pl.ds(2048 * k + c0 * 16, 512), :] = value
                    flat_f[pl.ds(2048 * k + c0 * 16, 512), :] = pixels - value
                return carry

            lax.fori_loop(0, 4, coarse_some, 0)

            def turn_some(k, carry, j=j, h=h):
                for y0 in range(0, 16, 4):
                    for band, flat in ((0, flat_c), (1, flat_f)):
                        lines = []
                        for y in range(y0, y0 + 4):
                            line = flat[pl.ds(2048 * k + y, 128, stride=16), :].astype(jnp.bfloat16)
                            bands_ref[CHUNK * j + 32 * h + 16 * k + y, 128 * band:128 * band + 128, :] = line
                            lines.append(line)
                        wide = jnp.concatenate(lines, axis=1)
                        grams[band] = grams[band] + lax.dot_general(
                            wide, wide, NT, preferred_element_type=jnp.float32)
                return carry

            lax.fori_loop(0, 2, turn_some, 0)

    flag = jnp.where(lax.broadcasted_iota(jnp.int32, (8, 128), 0) == region_ref[0, 0], 1.0, 0.0)
    for q in range(PLANE):
        pieces[q, 0] = grams[0, 8 * q:8 * q + 8, :]
        pieces[q, 1] = grams[1, 8 * q:8 * q + 8, :]
        pieces[q, 2] = flag
    one = []
    for step in range(1, PLANE):
        one.append(pltpu.make_async_remote_copy(
            src_ref=pieces.at[lax.rem(part + step, PLANE)], dst_ref=first.at[step],
            send_sem=s1.at[step], recv_sem=r1.at[step],
            device_id=plane_peer(step), device_id_type=MESH))
    for copy in one:
        copy.start()
    first[0] = pieces[part]
    for copy in one:
        copy.wait_recv()
    for region in range(8):
        total0 = jnp.zeros((8, 128), jnp.float32)
        total1 = jnp.zeros((8, 128), jnp.float32)
        for step in range(PLANE):
            flag = first[step, 2, region:region + 1, :]
            total0 = total0 + flag * first[step, 0]
            total1 = total1 + flag * first[step, 1]
        slots[region, 0] = total0
        slots[region, 1] = total1

    two = []
    for step in range(1, GROUP):
        two.append(pltpu.make_async_remote_copy(
            src_ref=slots, dst_ref=others.at[step],
            send_sem=s2.at[step], recv_sem=r2.at[step],
            device_id=group_peer(step), device_id_type=MESH))
    for copy in two:
        copy.start()
    for copy in two:
        copy.wait_recv()
    sums = []
    for region in range(8):
        pair = []
        for band in range(2):
            total = slots[region, band]
            for step in range(1, GROUP):
                total = total + others[step, region, band]
            pair.append(total)
        sums.append(pair)

    for step in range(PLANE):
        for band in range(2):
            total = jnp.zeros((8, 128), jnp.float32)
            for region in range(8):
                total = total + first[step, 2, region:region + 1, :] * sums[region][band]
            picked[step, band] = total
    three = []
    for step in range(1, PLANE):
        back = lax.rem(part + PLANE - step, PLANE)
        three.append(pltpu.make_async_remote_copy(
            src_ref=picked.at[step], dst_ref=last.at[part],
            send_sem=s3.at[step], recv_sem=r3.at[step],
            device_id=(row, half * PLANE + back), device_id_type=MESH))
    for copy in three:
        copy.start()
    last[part] = picked[0]
    for step in range(1, PLANE):
        ahead = lax.rem(part + step, PLANE)
        pltpu.make_async_remote_copy(
            src_ref=picked.at[step], dst_ref=last.at[ahead],
            send_sem=s3.at[step], recv_sem=r3.at[step],
            device_id=(row, half * PLANE + ahead), device_id_type=MESH).wait_recv()
    for index in range(PLANE):
        for band in range(2):
            gram_ref[band, index * 8:index * 8 + 8, :] = last[index, band]

    @pl.when(row < 3)
    def _():
        to_next.wait_send()

    @pl.when(row > 0)
    def _():
        to_last.wait_send()

    @pl.when(col < 31)
    def _():
        for j in range(4):
            to_right(j).wait_send()

    @pl.when(col > 0)
    def _():
        for j in range(4):
            to_left(j).wait_send()

    for copy in one + two + three:
        copy.wait_send()


def front(widths, region, sky):
    bf, f32 = jnp.bfloat16, jnp.float32
    dma = pltpu.SemaphoreType.DMA
    return pl.pallas_call(
        front_kernel,
        out_shape=(pltpu.VMEM((256, 256, 128), bf), pltpu.VMEM((2, 128, 128), f32)),
        in_specs=[pl.BlockSpec(memory_space=pltpu.SMEM)] * 2 + [pl.BlockSpec(memory_space=pl.ANY)],
        out_specs=(pl.BlockSpec(memory_space=pltpu.VMEM), pl.BlockSpec(memory_space=pltpu.VMEM)),
        scratch_shapes=[
            pltpu.VMEM((256, 128), bf),
            pltpu.VMEM((CHANS, 256 + 2 * HW, 128), bf),
            pltpu.VMEM((4, CHANS, CHUNK, 128), bf),
            pltpu.VMEM((4, CHANS, 16, 128), bf),
            pltpu.VMEM((4, CHANS, 16, 128), bf),
            pltpu.VMEM((4, CHANS, 16, 128), bf),
            pltpu.VMEM((4, CHANS, 16, 128), bf),
            pltpu.VMEM((2, 512, 256), bf),
            pltpu.VMEM((512, 256), bf),
            pltpu.VMEM((4096, 128), f32),
            pltpu.VMEM((4096, 128), f32),
            pltpu.VMEM((2, 128, 128), f32),
            pltpu.VMEM((PLANE, 3, 8, 128), f32),
            pltpu.VMEM((PLANE, 3, 8, 128), f32),
            pltpu.VMEM((8, 2, 8, 128), f32),
            pltpu.VMEM((GROUP, 8, 2, 8, 128), f32),
            pltpu.VMEM((PLANE, 2, 8, 128), f32),
            pltpu.VMEM((PLANE, 2, 8, 128), f32),
            pltpu.SemaphoreType.REGULAR,
            dma, dma((2,)), dma((2,)), dma((2, 4)), dma((2, 4)),
            dma((PLANE,)), dma((PLANE,)), dma((GROUP,)), dma((GROUP,)), dma((PLANE,)), dma((PLANE,)),
        ],
        compiler_params=pltpu.CompilerParams(
            collective_id=1, has_side_effects=True, vmem_limit_bytes=40 * 1024 * 1024),
        name="front",
    )(widths, region, sky)


WIDE = 4


def weights_of(grams, priors, cheb_t, keep):
    lanes = lax.broadcasted_iota(jnp.int32, (8, 128), 1)
    subs = lax.broadcasted_iota(jnp.int32, (8, 128), 0)
    mats = []
    for band in range(2):
        blocks = []
        for i in range(16):
            block = grams[band][i * 8:i * 8 + 8, :]
            diag = jnp.where(lanes == subs + 8 * i, priors[band], 0.0)
            blocks.append(block / 524288.0 + diag)
        blocks.append(cheb_t)
        mats.append(blocks)
    for k in range(0, 128, WIDE):
        at, off = k // 8, k % 8
        for band in range(2):
            m = mats[band]
            cols = [[jnp.broadcast_to(b[:, k + p:k + p + 1], (8, 128)) for b in m] for p in range(WIDE)]
            hit = (lanes >= k) & (lanes < k + WIDE)
            rows = [jnp.where(hit[0:1], jnp.where(lanes[0:1] == k + i, -1.0, 0.0), m[at][off + i:off + i + 1, :])
                    for i in range(WIDE)]
            d = [[cols[p][at][off + i:off + i + 1, :] for p in range(WIDE)] for i in range(WIDE)]
            inv = []
            for i in range(WIDE):
                inv.append(1.0 / d[i][i])
                for l in range(i + 1, WIDE):
                    t = d[l][i] * inv[i]
                    rows[l] = rows[l] - t * rows[i]
                    for j in range(i + 1, WIDE):
                        d[l][j] = d[l][j] - t * d[i][j]
            for i in reversed(range(WIDE)):
                line = rows[i]
                for j in range(i + 1, WIDE):
                    line = line - d[i][j] * rows[j]
                rows[i] = line * inv[i]
            fresh = []
            for index, b in enumerate(m):
                b = jnp.where(hit, 0.0, b)
                for p in range(WIDE):
                    b = b - cols[p][index] * rows[p]
                fresh.append(b)
            mats[band] = fresh
    out = []
    for band in range(2):
        mixed = mats[band][16] * keep
        kept = cheb_t * keep
        small = lax.dot_general(kept, mixed, (((1,), (1,)), ((), ())), precision=HIGH,
                                preferred_element_type=jnp.float32)
        eye = (lax.broadcasted_iota(jnp.int32, (8, 8), 0) == lax.broadcasted_iota(jnp.int32, (8, 8), 1))
        small = small + jnp.where(eye, 1.0 - keep[:, 0:8], 0.0)
        out.append((small, mixed))
    weights = []
    for small, mixed in out:
        for k in range(8):
            fac = small[:, k:k + 1]
            inv = 1.0 / fac[k:k + 1, :]
            shift = jnp.where(subs[:, 0:1] == k, 1.0, 0.0)
            fac = fac - shift
            srow = small[k:k + 1, :] * inv
            mrow = mixed[k:k + 1, :] * inv
            small = small - fac * srow
            mixed = mixed - fac * mrow
        weights.append(mixed)
    return weights


def chebyshev_rows():
    lane = lax.broadcasted_iota(jnp.int32, (8, 128), 1).astype(jnp.float32)
    order = lax.broadcasted_iota(jnp.int32, (8, 128), 0)
    position = (2.0 * lane + 1.0) / CHANS - 1.0
    terms = [jnp.ones_like(position), position]
    rows = jnp.where(order == 0, terms[0], position)
    for m in range(2, MMAX):
        terms.append(2.0 * position * terms[-1] - terms[-2])
        rows = jnp.where(order == m, terms[-1], rows)
    return rows


def back_kernel(region_ref, rank_ref, gram_ref, prior_ref, bands_ref, out_ref, proj, flat, ready, sems):
    cheb_t = chebyshev_rows()
    rank = rank_ref[region_ref[0, 0]]
    keep = jnp.where(lax.broadcasted_iota(jnp.int32, (8, 128), 0) < rank, 1.0, 0.0)
    weights = weights_of([gram_ref[0], gram_ref[1]], [prior_ref[0:1, :], prior_ref[1:2, :]], cheb_t, keep)
    kept = cheb_t * keep
    for band in range(2):
        part = lax.dot_general(kept, weights[band], (((0,), (0,)), ((), ())), precision=HIGH,
                               preferred_element_type=jnp.float32)
        proj[:, 128 * band:128 * band + 128] = part.astype(jnp.bfloat16)

    def put(slot, base):
        return pltpu.make_async_copy(ready.at[slot], out_ref.at[:, pl.ds(base, 16), :], sems.at[slot])

    def block(step, carry):
        for slot in range(2):
            base = pl.multiple_of(step * 32 + slot * 16, 16)
            for y in range(0, 16, 2):
                pair = jnp.concatenate([bands_ref[base + y], bands_ref[base + y + 1]], axis=1)
                removed = jnp.dot(proj[...], pair, preferred_element_type=jnp.float32)
                wide = pair.astype(jnp.float32)
                result = wide[0:128] + wide[128:256] - removed
                flat[pl.ds(2048 * slot + y, 128, stride=16), :] = result[:, 0:128]
                flat[pl.ds(2048 * slot + y + 1, 128, stride=16), :] = result[:, 128:256]

            @pl.when(step > 0)
            def _(slot=slot):
                put(slot, 0).wait()

            ready[slot] = flat[2048 * slot:2048 * slot + 2048, :].reshape(128, 16, 128).astype(jnp.bfloat16)
            put(slot, base).start()
        return carry

    lax.fori_loop(0, 8, block, 0)
    put(0, 0).wait()
    put(1, 0).wait()


def back(region, ranks, grams, prior_var, bands):
    whole = pl.BlockSpec(memory_space=pltpu.VMEM)
    bands = pltpu.with_memory_space_constraint(bands, pltpu.VMEM)
    return pl.pallas_call(
        back_kernel,
        out_shape=jax.ShapeDtypeStruct((128, 256, 128), jnp.bfloat16),
        in_specs=[pl.BlockSpec(memory_space=pltpu.SMEM)] * 2 + [whole] * 3,
        out_specs=pl.BlockSpec(memory_space=pl.ANY),
        scratch_shapes=[pltpu.VMEM((128, 256), jnp.bfloat16), pltpu.VMEM((4096, 128), jnp.float32),
                        pltpu.VMEM((2, 128, 16, 128), jnp.bfloat16), pltpu.SemaphoreType.DMA((2,))],
        compiler_params=pltpu.CompilerParams(vmem_limit_bytes=16 * 1024 * 1024),
        name="back",
    )(region, ranks, grams, prior_var, bands)


def local(sky, kernel_widths, prior_var, tile_region, region_rank):
    bands, own_gram = front(kernel_widths, tile_region, sky)
    return back(tile_region, region_rank, own_gram, prior_var, bands)


def solution(mesh):
    return jax.shard_map(
        local,
        mesh=mesh,
        in_specs=(P(None, "row", "col"), P(), P(), P("row", "col"), P()),
        out_specs=P(None, "row", "col"),
        check_vma=False,
    )
```

```python
import math
import jax
import jax.numpy as jnp
from jax import lax
from jax.experimental import pallas as pl
from jax.experimental.pallas import tpu as pltpu
from jax.sharding import PartitionSpec as P

HW = 32
MMAX = 8
TPR = 16
PLANE = 16
GROUP = 8
CHANS = 128
CHUNK = 64
ORDER = (1, 2, 0, 3)
MESH = pl.DeviceIdType.MESH
HIGH = lax.Precision.HIGHEST
NT = (((1,), (1,)), ((), ()))


def taps_table(down_width, across_width):
    line = lax.broadcasted_iota(jnp.int32, (256, 128), 0)
    lane = lax.broadcasted_iota(jnp.int32, (256, 128), 1)
    first = line < 192
    offsets = jnp.where(first, line - lane - HW, lane - (line - 192) - HW).astype(jnp.float32)
    spread = jnp.where(first, across_width, down_width).astype(jnp.float32)
    values = (1.0 + jnp.cos(math.pi * offsets / (spread + 1.0))) / (2.0 * spread + 2.0)
    return jnp.where(jnp.abs(offsets) <= spread, values, 0.0).astype(jnp.bfloat16)


def front_kernel(widths_ref, region_ref, sky_ref, bands_ref, gram_ref,
                 table_ref, skyx, smooth, out_l, out_r, in_l, in_r, across, pick, flat_c, flat_f, grams, pieces,
                 first, slots, others, picked, last,
                 go, sky_sem, ys, yr, xs, xr, s1, r1, s2, r2, s3, r3):
    row = lax.axis_index("row")
    col = lax.axis_index("col")
    part = lax.rem(col, PLANE)
    half = lax.div(col, PLANE)
    place = half * 4 + row

    def plane_peer(step):
        return (row, half * PLANE + lax.rem(part + step, PLANE))

    def group_peer(step):
        other = lax.rem(place + step, GROUP)
        return (lax.rem(other, 4), lax.div(other, 4) * PLANE + part)

    barrier = pltpu.get_barrier_semaphore()
    for step in (1, 31):
        pl.semaphore_signal(barrier, inc=1, device_id=(row, lax.rem(col + step, 32)), device_id_type=MESH)
    for step in range(1, GROUP):
        pl.semaphore_signal(barrier, inc=1, device_id=group_peer(step), device_id_type=MESH)
    for step in range(1, PLANE):
        pl.semaphore_signal(barrier, inc=1, device_id=plane_peer(step), device_id_type=MESH)

    load = pltpu.make_async_copy(sky_ref, skyx.at[:, HW:HW + 256, :], sky_sem)
    load.start()

    table_ref[...] = taps_table(widths_ref[0], widths_ref[1])

    zero = jnp.zeros((512, 256), jnp.bfloat16)
    own = table_ref[HW:HW + 128, :]
    for h in range(2):
        across[h] = zero
        across[h, 0:128, 0:128] = own
        across[h, 128:256, 128:256] = own
        for k in range(2):
            base = HW * (2 * h + k)
            across[h, 256 + base:256 + base + HW, 128 * k:128 * k + 128] = table_ref[0:HW, :]
            across[h, 384 + base:384 + base + HW, 128 * k:128 * k + 128] = table_ref[160:192, :]
    source = lax.broadcasted_iota(jnp.int32, (512, 256), 0)
    target = lax.broadcasted_iota(jnp.int32, (512, 256), 1)
    lane = target % 128
    wanted = (lane // HW) * 128 + lane % HW + jnp.where(target >= 128, 96, 0)
    pick[...] = jnp.where(source == wanted, 1.0, 0.0).astype(jnp.bfloat16)
    down = table_ref[192:256, :]
    grams[...] = jnp.zeros((2, 128, 128), jnp.float32)

    @pl.when(row == 0)
    def _():
        skyx[:, 0:HW, :] = jnp.zeros((CHANS, HW, 128), jnp.bfloat16)

    @pl.when(row == 3)
    def _():
        skyx[:, HW + 256:, :] = jnp.zeros((CHANS, HW, 128), jnp.bfloat16)

    @pl.when(col == 0)
    def _():
        in_l[...] = jnp.zeros(in_l.shape, jnp.bfloat16)

    @pl.when(col == 31)
    def _():
        in_r[...] = jnp.zeros(in_r.shape, jnp.bfloat16)

    to_next = pltpu.make_async_remote_copy(
        src_ref=sky_ref.at[:, 256 - HW:256, :], dst_ref=skyx.at[:, 0:HW, :],
        send_sem=ys.at[0], recv_sem=yr.at[0], device_id=(lax.rem(row + 1, 4), col), device_id_type=MESH)
    to_last = pltpu.make_async_remote_copy(
        src_ref=sky_ref.at[:, 0:HW, :], dst_ref=skyx.at[:, HW + 256:, :],
        send_sem=ys.at[1], recv_sem=yr.at[1], device_id=(lax.rem(row + 3, 4), col), device_id_type=MESH)

    def to_right(j):
        return pltpu.make_async_remote_copy(
            src_ref=out_r.at[j], dst_ref=in_l.at[j], send_sem=xs.at[0, j], recv_sem=xr.at[0, j],
            device_id=(row, lax.rem(col + 1, 32)), device_id_type=MESH)

    def to_left(j):
        return pltpu.make_async_remote_copy(
            src_ref=out_l.at[j], dst_ref=in_r.at[j], send_sem=xs.at[1, j], recv_sem=xr.at[1, j],
            device_id=(row, lax.rem(col + 31, 32)), device_id_type=MESH)

    def smooth_chunk(j):
        def smooth_some(step, carry):
            c0 = step * 16
            for p in range(8):
                c = c0 + 2 * p
                window = jnp.concatenate(
                    [skyx[c, CHUNK * j:CHUNK * j + 128, :], skyx[c + 1, CHUNK * j:CHUNK * j + 128, :]], axis=1)
                result = jnp.dot(down, window, preferred_element_type=jnp.float32).astype(jnp.bfloat16)
                smooth[j, c] = result[:, 0:128]
                smooth[j, c + 1] = result[:, 128:256]
            return carry

        lax.fori_loop(0, 8, smooth_some, 0)

    def pack_chunk(j):
        def pack_some(step, carry):
            c0 = step * 32
            wide = jnp.concatenate(
                [smooth[j, pl.ds(c0, 32), 16 * q:16 * q + 16, :].reshape(512, 128) for q in range(4)], axis=1)
            edges = jnp.dot(wide, pick[...], preferred_element_type=jnp.float32).astype(jnp.bfloat16)
            out_l[j, pl.ds(c0, 32)] = edges[:, 0:128].reshape(32, 16, 128)
            out_r[j, pl.ds(c0, 32)] = edges[:, 128:256].reshape(32, 16, 128)
            return carry

        lax.fori_loop(0, 4, pack_some, 0)

    load.wait()
    for j in ORDER:
        if j == ORDER[2]:
            @pl.when(row > 0)
            def _():
                to_next.wait_recv()

            @pl.when(row < 3)
            def _():
                to_last.wait_recv()

            middle = (row == 1) | (row == 2)
            crossing = (col == 15) | (col == 16)

            @pl.when(middle & (col == 12))
            def _():
                pl.semaphore_signal(go, inc=1, device_id=(row, col + 3), device_id_type=MESH)

            @pl.when(middle & (col == 19))
            def _():
                pl.semaphore_signal(go, inc=1, device_id=(row, col - 3), device_id_type=MESH)

            @pl.when(crossing)
            def _():
                pl.semaphore_wait(go, 1)

            @pl.when(middle & crossing)
            def _():
                pl.semaphore_signal(go, inc=1, device_id=((row - 1) * 3, col), device_id_type=MESH)

            @pl.when(col == 15)
            def _():
                to_right(ORDER[1]).start()

            @pl.when(col == 16)
            def _():
                to_left(ORDER[1]).start()

        smooth_chunk(j)
        if j == ORDER[0]:
            pl.semaphore_wait(barrier, PLANE + GROUP)

            @pl.when(row < 3)
            def _():
                to_next.start()

            @pl.when(row > 0)
            def _():
                to_last.start()

        pack_chunk(j)
        late = j != ORDER[1]

        @pl.when((col < 31) & (late | (col != 15)))
        def _(j=j):
            to_right(j).start()

        @pl.when((col > 0) & (late | (col != 16)))
        def _(j=j):
            to_left(j).start()

    for j in ORDER:
        @pl.when(col > 0)
        def _(j=j):
            to_right(j).wait_recv()

        @pl.when(col < 31)
        def _(j=j):
            to_left(j).wait_recv()

        for h in range(2):
            def coarse_some(step, carry, j=j, h=h):
                c0 = step * 32
                wide = jnp.concatenate(
                    [smooth[j, pl.ds(c0, 32), 32 * h + 16 * k:32 * h + 16 * k + 16, :].reshape(512, 128)
                     for k in range(2)]
                    + [in_l[j, pl.ds(c0, 32)].reshape(512, 128), in_r[j, pl.ds(c0, 32)].reshape(512, 128)], axis=1)
                both = jnp.dot(wide, across[h], preferred_element_type=jnp.float32)
                both = both.astype(jnp.bfloat16).astype(jnp.float32)
                for k in range(2):
                    begin = HW + CHUNK * j + 32 * h + 16 * k
                    value = both[:, 128 * k:128 * k + 128]
                    pixels = skyx[pl.ds(c0, 32), begin:begin + 16, :].reshape(512, 128).astype(jnp.float32)
                    flat_c[pl.ds(2048 * k + c0 * 16, 512), :] = value
                    flat_f[pl.ds(2048 * k + c0 * 16, 512), :] = pixels - value
                return carry

            lax.fori_loop(0, 4, coarse_some, 0)

            def turn_some(k, carry, j=j, h=h):
                for y0 in range(0, 16, 4):
                    for band, flat in ((0, flat_c), (1, flat_f)):
                        lines = []
                        for y in range(y0, y0 + 4):
                            line = flat[pl.ds(2048 * k + y, 128, stride=16), :].astype(jnp.bfloat16)
                            bands_ref[CHUNK * j + 32 * h + 16 * k + y, 128 * band:128 * band + 128, :] = line
                            lines.append(line)
                        wide = jnp.concatenate(lines, axis=1)
                        grams[band] = grams[band] + lax.dot_general(
                            wide, wide, NT, preferred_element_type=jnp.float32)
                return carry

            lax.fori_loop(0, 2, turn_some, 0)

    flag = jnp.where(lax.broadcasted_iota(jnp.int32, (8, 128), 0) == region_ref[0, 0], 1.0, 0.0)
    for q in range(PLANE):
        pieces[q, 0] = grams[0, 8 * q:8 * q + 8, :]
        pieces[q, 1] = grams[1, 8 * q:8 * q + 8, :]
        pieces[q, 2] = flag
    one = []
    for step in range(1, PLANE):
        one.append(pltpu.make_async_remote_copy(
            src_ref=pieces.at[lax.rem(part + step, PLANE)], dst_ref=first.at[step],
            send_sem=s1.at[step], recv_sem=r1.at[step],
            device_id=plane_peer(step), device_id_type=MESH))
    for copy in one:
        copy.start()
    first[0] = pieces[part]
    for copy in one:
        copy.wait_recv()
    for region in range(8):
        total0 = jnp.zeros((8, 128), jnp.float32)
        total1 = jnp.zeros((8, 128), jnp.float32)
        for step in range(PLANE):
            flag = first[step, 2, region:region + 1, :]
            total0 = total0 + flag * first[step, 0]
            total1 = total1 + flag * first[step, 1]
        slots[region, 0] = total0
        slots[region, 1] = total1

    two = []
    for step in range(1, GROUP):
        two.append(pltpu.make_async_remote_copy(
            src_ref=slots, dst_ref=others.at[step],
            send_sem=s2.at[step], recv_sem=r2.at[step],
            device_id=group_peer(step), device_id_type=MESH))
    for copy in two:
        copy.start()
    for copy in two:
        copy.wait_recv()
    sums = []
    for region in range(8):
        pair = []
        for band in range(2):
            total = slots[region, band]
            for step in range(1, GROUP):
                total = total + others[step, region, band]
            pair.append(total)
        sums.append(pair)

    for step in range(PLANE):
        for band in range(2):
            total = jnp.zeros((8, 128), jnp.float32)
            for region in range(8):
                total = total + first[step, 2, region:region + 1, :] * sums[region][band]
            picked[step, band] = total
    three = []
    for step in range(1, PLANE):
        back = lax.rem(part + PLANE - step, PLANE)
        three.append(pltpu.make_async_remote_copy(
            src_ref=picked.at[step], dst_ref=last.at[part],
            send_sem=s3.at[step], recv_sem=r3.at[step],
            device_id=(row, half * PLANE + back), device_id_type=MESH))
    for copy in three:
        copy.start()
    last[part] = picked[0]
    for step in range(1, PLANE):
        ahead = lax.rem(part + step, PLANE)
        pltpu.make_async_remote_copy(
            src_ref=picked.at[step], dst_ref=last.at[ahead],
            send_sem=s3.at[step], recv_sem=r3.at[step],
            device_id=(row, half * PLANE + ahead), device_id_type=MESH).wait_recv()
    for index in range(PLANE):
        for band in range(2):
            gram_ref[band, index * 8:index * 8 + 8, :] = last[index, band]

    @pl.when(row < 3)
    def _():
        to_next.wait_send()

    @pl.when(row > 0)
    def _():
        to_last.wait_send()

    @pl.when(col < 31)
    def _():
        for j in ORDER:
            to_right(j).wait_send()

    @pl.when(col > 0)
    def _():
        for j in ORDER:
            to_left(j).wait_send()

    for copy in one + two + three:
        copy.wait_send()


def front(widths, region, sky):
    bf, f32 = jnp.bfloat16, jnp.float32
    dma = pltpu.SemaphoreType.DMA
    return pl.pallas_call(
        front_kernel,
        out_shape=(pltpu.VMEM((256, 256, 128), bf), pltpu.VMEM((2, 128, 128), f32)),
        in_specs=[pl.BlockSpec(memory_space=pltpu.SMEM)] * 2 + [pl.BlockSpec(memory_space=pl.ANY)],
        out_specs=(pl.BlockSpec(memory_space=pltpu.VMEM), pl.BlockSpec(memory_space=pltpu.VMEM)),
        scratch_shapes=[
            pltpu.VMEM((256, 128), bf),
            pltpu.VMEM((CHANS, 256 + 2 * HW, 128), bf),
            pltpu.VMEM((4, CHANS, CHUNK, 128), bf),
            pltpu.VMEM((4, CHANS, 16, 128), bf),
            pltpu.VMEM((4, CHANS, 16, 128), bf),
            pltpu.VMEM((4, CHANS, 16, 128), bf),
            pltpu.VMEM((4, CHANS, 16, 128), bf),
            pltpu.VMEM((2, 512, 256), bf),
            pltpu.VMEM((512, 256), bf),
            pltpu.VMEM((4096, 128), f32),
            pltpu.VMEM((4096, 128), f32),
            pltpu.VMEM((2, 128, 128), f32),
            pltpu.VMEM((PLANE, 3, 8, 128), f32),
            pltpu.VMEM((PLANE, 3, 8, 128), f32),
            pltpu.VMEM((8, 2, 8, 128), f32),
            pltpu.VMEM((GROUP, 8, 2, 8, 128), f32),
            pltpu.VMEM((PLANE, 2, 8, 128), f32),
            pltpu.VMEM((PLANE, 2, 8, 128), f32),
            pltpu.SemaphoreType.REGULAR,
            dma, dma((2,)), dma((2,)), dma((2, 4)), dma((2, 4)),
            dma((PLANE,)), dma((PLANE,)), dma((GROUP,)), dma((GROUP,)), dma((PLANE,)), dma((PLANE,)),
        ],
        compiler_params=pltpu.CompilerParams(
            collective_id=1, has_side_effects=True, vmem_limit_bytes=40 * 1024 * 1024),
        name="front",
    )(widths, region, sky)


WIDE = 4


def weights_of(grams, priors, cheb_t, keep):
    lanes = lax.broadcasted_iota(jnp.int32, (8, 128), 1)
    subs = lax.broadcasted_iota(jnp.int32, (8, 128), 0)
    mats = []
    for band in range(2):
        blocks = []
        for i in range(16):
            block = grams[band][i * 8:i * 8 + 8, :]
            diag = jnp.where(lanes == subs + 8 * i, priors[band], 0.0)
            blocks.append(block / 524288.0 + diag)
        blocks.append(cheb_t)
        mats.append(blocks)
    for k in range(0, 128, WIDE):
        at, off = k // 8, k % 8
        for band in range(2):
            m = mats[band]
            cols = [[jnp.broadcast_to(b[:, k + p:k + p + 1], (8, 128)) for b in m] for p in range(WIDE)]
            hit = (lanes >= k) & (lanes < k + WIDE)
            rows = [jnp.where(hit[0:1], jnp.where(lanes[0:1] == k + i, -1.0, 0.0), m[at][off + i:off + i + 1, :])
                    for i in range(WIDE)]
            d = [[cols[p][at][off + i:off + i + 1, :] for p in range(WIDE)] for i in range(WIDE)]
            inv = []
            for i in range(WIDE):
                inv.append(1.0 / d[i][i])
                for l in range(i + 1, WIDE):
                    t = d[l][i] * inv[i]
                    rows[l] = rows[l] - t * rows[i]
                    for j in range(i + 1, WIDE):
                        d[l][j] = d[l][j] - t * d[i][j]
            for i in reversed(range(WIDE)):
                line = rows[i]
                for j in range(i + 1, WIDE):
                    line = line - d[i][j] * rows[j]
                rows[i] = line * inv[i]
            fresh = []
            for index, b in enumerate(m):
                b = jnp.where(hit, 0.0, b)
                for p in range(WIDE):
                    b = b - cols[p][index] * rows[p]
                fresh.append(b)
            mats[band] = fresh
    out = []
    for band in range(2):
        mixed = mats[band][16] * keep
        kept = cheb_t * keep
        small = lax.dot_general(kept, mixed, (((1,), (1,)), ((), ())), precision=HIGH,
                                preferred_element_type=jnp.float32)
        eye = (lax.broadcasted_iota(jnp.int32, (8, 8), 0) == lax.broadcasted_iota(jnp.int32, (8, 8), 1))
        small = small + jnp.where(eye, 1.0 - keep[:, 0:8], 0.0)
        out.append((small, mixed))
    weights = []
    for small, mixed in out:
        for k in range(8):
            fac = small[:, k:k + 1]
            inv = 1.0 / fac[k:k + 1, :]
            shift = jnp.where(subs[:, 0:1] == k, 1.0, 0.0)
            fac = fac - shift
            srow = small[k:k + 1, :] * inv
            mrow = mixed[k:k + 1, :] * inv
            small = small - fac * srow
            mixed = mixed - fac * mrow
        weights.append(mixed)
    return weights


def chebyshev_rows():
    lane = lax.broadcasted_iota(jnp.int32, (8, 128), 1).astype(jnp.float32)
    order = lax.broadcasted_iota(jnp.int32, (8, 128), 0)
    position = (2.0 * lane + 1.0) / CHANS - 1.0
    terms = [jnp.ones_like(position), position]
    rows = jnp.where(order == 0, terms[0], position)
    for m in range(2, MMAX):
        terms.append(2.0 * position * terms[-1] - terms[-2])
        rows = jnp.where(order == m, terms[-1], rows)
    return rows


def back_kernel(region_ref, rank_ref, gram_ref, prior_ref, bands_ref, out_ref, proj, flat, ready, sems):
    cheb_t = chebyshev_rows()
    rank = rank_ref[region_ref[0, 0]]
    keep = jnp.where(lax.broadcasted_iota(jnp.int32, (8, 128), 0) < rank, 1.0, 0.0)
    weights = weights_of([gram_ref[0], gram_ref[1]], [prior_ref[0:1, :], prior_ref[1:2, :]], cheb_t, keep)
    kept = cheb_t * keep
    for band in range(2):
        part = lax.dot_general(kept, weights[band], (((0,), (0,)), ((), ())), precision=HIGH,
                               preferred_element_type=jnp.float32)
        proj[:, 128 * band:128 * band + 128] = part.astype(jnp.bfloat16)

    def put(slot, base):
        return pltpu.make_async_copy(ready.at[slot], out_ref.at[:, pl.ds(base, 16), :], sems.at[slot])

    def block(step, carry):
        for slot in range(2):
            base = pl.multiple_of(step * 32 + slot * 16, 16)
            for y in range(0, 16, 2):
                pair = jnp.concatenate([bands_ref[base + y], bands_ref[base + y + 1]], axis=1)
                removed = jnp.dot(proj[...], pair, preferred_element_type=jnp.float32)
                wide = pair.astype(jnp.float32)
                result = wide[0:128] + wide[128:256] - removed
                flat[pl.ds(2048 * slot + y, 128, stride=16), :] = result[:, 0:128]
                flat[pl.ds(2048 * slot + y + 1, 128, stride=16), :] = result[:, 128:256]

            @pl.when(step > 0)
            def _(slot=slot):
                put(slot, 0).wait()

            ready[slot] = flat[2048 * slot:2048 * slot + 2048, :].reshape(128, 16, 128).astype(jnp.bfloat16)
            put(slot, base).start()
        return carry

    lax.fori_loop(0, 8, block, 0)
    put(0, 0).wait()
    put(1, 0).wait()


def back(region, ranks, grams, prior_var, bands):
    whole = pl.BlockSpec(memory_space=pltpu.VMEM)
    bands = pltpu.with_memory_space_constraint(bands, pltpu.VMEM)
    return pl.pallas_call(
        back_kernel,
        out_shape=jax.ShapeDtypeStruct((128, 256, 128), jnp.bfloat16),
        in_specs=[pl.BlockSpec(memory_space=pltpu.SMEM)] * 2 + [whole] * 3,
        out_specs=pl.BlockSpec(memory_space=pl.ANY),
        scratch_shapes=[pltpu.VMEM((128, 256), jnp.bfloat16), pltpu.VMEM((4096, 128), jnp.float32),
                        pltpu.VMEM((2, 128, 16, 128), jnp.bfloat16), pltpu.SemaphoreType.DMA((2,))],
        compiler_params=pltpu.CompilerParams(vmem_limit_bytes=16 * 1024 * 1024),
        name="back",
    )(region, ranks, grams, prior_var, bands)


def local(sky, kernel_widths, prior_var, tile_region, region_rank):
    bands, own_gram = front(kernel_widths, tile_region, sky)
    return back(tile_region, region_rank, own_gram, prior_var, bands)


def solution(mesh):
    return jax.shard_map(
        local,
        mesh=mesh,
        in_specs=(P(None, "row", "col"), P(), P(), P("row", "col"), P()),
        out_specs=P(None, "row", "col"),
        check_vma=False,
    )
```

```python
import math
import jax
import jax.numpy as jnp
from jax import lax
from jax.experimental import pallas as pl
from jax.experimental.pallas import tpu as pltpu
from jax.sharding import PartitionSpec as P

HW = 32
MMAX = 8
TPR = 16
PLANE = 16
GROUP = 8
CHANS = 128
CHUNK = 64
ORDER = (1, 2, 0, 3)
MESH = pl.DeviceIdType.MESH
HIGH = lax.Precision.HIGHEST
NT = (((1,), (1,)), ((), ()))


def taps_table(down_width, across_width):
    line = lax.broadcasted_iota(jnp.int32, (256, 128), 0)
    lane = lax.broadcasted_iota(jnp.int32, (256, 128), 1)
    first = line < 192
    offsets = jnp.where(first, line - lane - HW, lane - (line - 192) - HW).astype(jnp.float32)
    spread = jnp.where(first, across_width, down_width).astype(jnp.float32)
    values = (1.0 + jnp.cos(math.pi * offsets / (spread + 1.0))) / (2.0 * spread + 2.0)
    return jnp.where(jnp.abs(offsets) <= spread, values, 0.0).astype(jnp.bfloat16)


def front_kernel(widths_ref, region_ref, sky_ref, bands_ref, gram_ref,
                 table_ref, skyx, smooth, out_l, out_r, in_l, in_r, across, pick, flat_c, flat_f, grams, pieces,
                 first, slots, others, picked, last,
                 go, sky_sem, ys, yr, xs, xr, s1, r1, s2, r2, s3, r3):
    row = lax.axis_index("row")
    col = lax.axis_index("col")
    part = lax.rem(col, PLANE)
    half = lax.div(col, PLANE)
    place = half * 4 + row

    def plane_peer(step):
        return (row, half * PLANE + lax.rem(part + step, PLANE))

    def group_peer(step):
        other = lax.rem(place + step, GROUP)
        return (lax.rem(other, 4), lax.div(other, 4) * PLANE + part)

    barrier = pltpu.get_barrier_semaphore()
    for step in (1, 31):
        pl.semaphore_signal(barrier, inc=1, device_id=(row, lax.rem(col + step, 32)), device_id_type=MESH)
    for step in range(1, GROUP):
        pl.semaphore_signal(barrier, inc=1, device_id=group_peer(step), device_id_type=MESH)
    for step in range(1, PLANE):
        pl.semaphore_signal(barrier, inc=1, device_id=plane_peer(step), device_id_type=MESH)

    load = pltpu.make_async_copy(sky_ref, skyx.at[:, HW:HW + 256, :], sky_sem)
    load.start()

    table_ref[...] = taps_table(widths_ref[0], widths_ref[1])

    zero = jnp.zeros((512, 256), jnp.bfloat16)
    own = table_ref[HW:HW + 128, :]
    for h in range(2):
        across[h] = zero
        across[h, 0:128, 0:128] = own
        across[h, 128:256, 128:256] = own
        for k in range(2):
            base = HW * (2 * h + k)
            across[h, 256 + base:256 + base + HW, 128 * k:128 * k + 128] = table_ref[0:HW, :]
            across[h, 384 + base:384 + base + HW, 128 * k:128 * k + 128] = table_ref[160:192, :]
    source = lax.broadcasted_iota(jnp.int32, (512, 256), 0)
    target = lax.broadcasted_iota(jnp.int32, (512, 256), 1)
    lane = target % 128
    wanted = (lane // HW) * 128 + lane % HW + jnp.where(target >= 128, 96, 0)
    pick[...] = jnp.where(source == wanted, 1.0, 0.0).astype(jnp.bfloat16)
    down = table_ref[192:256, :]
    grams[...] = jnp.zeros((2, 128, 128), jnp.float32)

    @pl.when(row == 0)
    def _():
        skyx[:, 0:HW, :] = jnp.zeros((CHANS, HW, 128), jnp.bfloat16)

    @pl.when(row == 3)
    def _():
        skyx[:, HW + 256:, :] = jnp.zeros((CHANS, HW, 128), jnp.bfloat16)

    @pl.when(col == 0)
    def _():
        in_l[...] = jnp.zeros(in_l.shape, jnp.bfloat16)

    @pl.when(col == 31)
    def _():
        in_r[...] = jnp.zeros(in_r.shape, jnp.bfloat16)

    to_next = pltpu.make_async_remote_copy(
        src_ref=sky_ref.at[:, 256 - HW:256, :], dst_ref=skyx.at[:, 0:HW, :],
        send_sem=ys.at[0], recv_sem=yr.at[0], device_id=(lax.rem(row + 1, 4), col), device_id_type=MESH)
    to_last = pltpu.make_async_remote_copy(
        src_ref=sky_ref.at[:, 0:HW, :], dst_ref=skyx.at[:, HW + 256:, :],
        send_sem=ys.at[1], recv_sem=yr.at[1], device_id=(lax.rem(row + 3, 4), col), device_id_type=MESH)

    def to_right(j):
        return pltpu.make_async_remote_copy(
            src_ref=out_r.at[j], dst_ref=in_l.at[j], send_sem=xs.at[0, j], recv_sem=xr.at[0, j],
            device_id=(row, lax.rem(col + 1, 32)), device_id_type=MESH)

    def to_left(j):
        return pltpu.make_async_remote_copy(
            src_ref=out_l.at[j], dst_ref=in_r.at[j], send_sem=xs.at[1, j], recv_sem=xr.at[1, j],
            device_id=(row, lax.rem(col + 31, 32)), device_id_type=MESH)

    def smooth_chunk(j):
        def smooth_some(step, carry):
            c0 = step * 16
            for p in range(8):
                c = c0 + 2 * p
                window = jnp.concatenate(
                    [skyx[c, CHUNK * j:CHUNK * j + 128, :], skyx[c + 1, CHUNK * j:CHUNK * j + 128, :]], axis=1)
                result = jnp.dot(down, window, preferred_element_type=jnp.float32).astype(jnp.bfloat16)
                smooth[j, c] = result[:, 0:128]
                smooth[j, c + 1] = result[:, 128:256]
            return carry

        lax.fori_loop(0, 8, smooth_some, 0)

    def pack_chunk(j):
        def pack_some(step, carry):
            c0 = step * 32
            wide = jnp.concatenate(
                [smooth[j, pl.ds(c0, 32), 16 * q:16 * q + 16, :].reshape(512, 128) for q in range(4)], axis=1)
            edges = jnp.dot(wide, pick[...], preferred_element_type=jnp.float32).astype(jnp.bfloat16)
            out_l[j, pl.ds(c0, 32)] = edges[:, 0:128].reshape(32, 16, 128)
            out_r[j, pl.ds(c0, 32)] = edges[:, 128:256].reshape(32, 16, 128)
            return carry

        lax.fori_loop(0, 4, pack_some, 0)

    pl.semaphore_wait(barrier, PLANE + GROUP)

    @pl.when(row < 3)
    def _():
        to_next.start()

    @pl.when(row > 0)
    def _():
        to_last.start()

    load.wait()
    for j in ORDER:
        if j == ORDER[2]:
            @pl.when(row > 0)
            def _():
                to_next.wait_recv()

            @pl.when(row < 3)
            def _():
                to_last.wait_recv()

            middle = (row == 1) | (row == 2)
            crossing = (col == 15) | (col == 16)

            @pl.when(middle & (col == 12))
            def _():
                pl.semaphore_signal(go, inc=1, device_id=(row, col + 3), device_id_type=MESH)

            @pl.when(middle & (col == 19))
            def _():
                pl.semaphore_signal(go, inc=1, device_id=(row, col - 3), device_id_type=MESH)

            @pl.when(crossing)
            def _():
                pl.semaphore_wait(go, 1)

            @pl.when(middle & crossing)
            def _():
                pl.semaphore_signal(go, inc=1, device_id=((row - 1) * 3, col), device_id_type=MESH)

            @pl.when(col == 15)
            def _():
                to_right(ORDER[1]).start()

            @pl.when(col == 16)
            def _():
                to_left(ORDER[1]).start()

        smooth_chunk(j)
        pack_chunk(j)
        late = j != ORDER[1]

        @pl.when((col < 31) & (late | (col != 15)))
        def _(j=j):
            to_right(j).start()

        @pl.when((col > 0) & (late | (col != 16)))
        def _(j=j):
            to_left(j).start()

    for j in ORDER:
        @pl.when(col > 0)
        def _(j=j):
            to_right(j).wait_recv()

        @pl.when(col < 31)
        def _(j=j):
            to_left(j).wait_recv()

        for h in range(2):
            def coarse_some(step, carry, j=j, h=h):
                c0 = step * 32
                wide = jnp.concatenate(
                    [smooth[j, pl.ds(c0, 32), 32 * h + 16 * k:32 * h + 16 * k + 16, :].reshape(512, 128)
                     for k in range(2)]
                    + [in_l[j, pl.ds(c0, 32)].reshape(512, 128), in_r[j, pl.ds(c0, 32)].reshape(512, 128)], axis=1)
                both = jnp.dot(wide, across[h], preferred_element_type=jnp.float32)
                both = both.astype(jnp.bfloat16).astype(jnp.float32)
                for k in range(2):
                    begin = HW + CHUNK * j + 32 * h + 16 * k
                    value = both[:, 128 * k:128 * k + 128]
                    pixels = skyx[pl.ds(c0, 32), begin:begin + 16, :].reshape(512, 128).astype(jnp.float32)
                    flat_c[pl.ds(2048 * k + c0 * 16, 512), :] = value
                    flat_f[pl.ds(2048 * k + c0 * 16, 512), :] = pixels - value
                return carry

            lax.fori_loop(0, 4, coarse_some, 0)

            def turn_some(k, carry, j=j, h=h):
                for y0 in range(0, 16, 4):
                    for band, flat in ((0, flat_c), (1, flat_f)):
                        lines = []
                        for y in range(y0, y0 + 4):
                            line = flat[pl.ds(2048 * k + y, 128, stride=16), :].astype(jnp.bfloat16)
                            bands_ref[CHUNK * j + 32 * h + 16 * k + y, 128 * band:128 * band + 128, :] = line
                            lines.append(line)
                        wide = jnp.concatenate(lines, axis=1)
                        grams[band] = grams[band] + lax.dot_general(
                            wide, wide, NT, preferred_element_type=jnp.float32)
                return carry

            lax.fori_loop(0, 2, turn_some, 0)

    flag = jnp.where(lax.broadcasted_iota(jnp.int32, (8, 128), 0) == region_ref[0, 0], 1.0, 0.0)
    for q in range(PLANE):
        pieces[q, 0] = grams[0, 8 * q:8 * q + 8, :]
        pieces[q, 1] = grams[1, 8 * q:8 * q + 8, :]
        pieces[q, 2] = flag
    one = []
    for step in range(1, PLANE):
        one.append(pltpu.make_async_remote_copy(
            src_ref=pieces.at[lax.rem(part + step, PLANE)], dst_ref=first.at[step],
            send_sem=s1.at[step], recv_sem=r1.at[step],
            device_id=plane_peer(step), device_id_type=MESH))
    for copy in one:
        copy.start()
    first[0] = pieces[part]
    for copy in one:
        copy.wait_recv()
    for region in range(8):
        total0 = jnp.zeros((8, 128), jnp.float32)
        total1 = jnp.zeros((8, 128), jnp.float32)
        for step in range(PLANE):
            flag = first[step, 2, region:region + 1, :]
            total0 = total0 + flag * first[step, 0]
            total1 = total1 + flag * first[step, 1]
        slots[region, 0] = total0
        slots[region, 1] = total1

    two = []
    for step in range(1, GROUP):
        two.append(pltpu.make_async_remote_copy(
            src_ref=slots, dst_ref=others.at[step],
            send_sem=s2.at[step], recv_sem=r2.at[step],
            device_id=group_peer(step), device_id_type=MESH))
    for copy in two:
        copy.start()
    for copy in two:
        copy.wait_recv()
    sums = []
    for region in range(8):
        pair = []
        for band in range(2):
            total = slots[region, band]
            for step in range(1, GROUP):
                total = total + others[step, region, band]
            pair.append(total)
        sums.append(pair)

    for step in range(PLANE):
        for band in range(2):
            total = jnp.zeros((8, 128), jnp.float32)
            for region in range(8):
                total = total + first[step, 2, region:region + 1, :] * sums[region][band]
            picked[step, band] = total
    three = []
    for step in range(1, PLANE):
        back = lax.rem(part + PLANE - step, PLANE)
        three.append(pltpu.make_async_remote_copy(
            src_ref=picked.at[step], dst_ref=last.at[part],
            send_sem=s3.at[step], recv_sem=r3.at[step],
            device_id=(row, half * PLANE + back), device_id_type=MESH))
    for copy in three:
        copy.start()
    last[part] = picked[0]
    for step in range(1, PLANE):
        ahead = lax.rem(part + step, PLANE)
        pltpu.make_async_remote_copy(
            src_ref=picked.at[step], dst_ref=last.at[ahead],
            send_sem=s3.at[step], recv_sem=r3.at[step],
            device_id=(row, half * PLANE + ahead), device_id_type=MESH).wait_recv()
    for index in range(PLANE):
        for band in range(2):
            gram_ref[band, index * 8:index * 8 + 8, :] = last[index, band]

    @pl.when(row < 3)
    def _():
        to_next.wait_send()

    @pl.when(row > 0)
    def _():
        to_last.wait_send()

    @pl.when(col < 31)
    def _():
        for j in ORDER:
            to_right(j).wait_send()

    @pl.when(col > 0)
    def _():
        for j in ORDER:
            to_left(j).wait_send()

    for copy in one + two + three:
        copy.wait_send()


def front(widths, region, sky):
    bf, f32 = jnp.bfloat16, jnp.float32
    dma = pltpu.SemaphoreType.DMA
    return pl.pallas_call(
        front_kernel,
        out_shape=(pltpu.VMEM((256, 256, 128), bf), pltpu.VMEM((2, 128, 128), f32)),
        in_specs=[pl.BlockSpec(memory_space=pltpu.SMEM)] * 2 + [pl.BlockSpec(memory_space=pl.ANY)],
        out_specs=(pl.BlockSpec(memory_space=pltpu.VMEM), pl.BlockSpec(memory_space=pltpu.VMEM)),
        scratch_shapes=[
            pltpu.VMEM((256, 128), bf),
            pltpu.VMEM((CHANS, 256 + 2 * HW, 128), bf),
            pltpu.VMEM((4, CHANS, CHUNK, 128), bf),
            pltpu.VMEM((4, CHANS, 16, 128), bf),
            pltpu.VMEM((4, CHANS, 16, 128), bf),
            pltpu.VMEM((4, CHANS, 16, 128), bf),
            pltpu.VMEM((4, CHANS, 16, 128), bf),
            pltpu.VMEM((2, 512, 256), bf),
            pltpu.VMEM((512, 256), bf),
            pltpu.VMEM((4096, 128), f32),
            pltpu.VMEM((4096, 128), f32),
            pltpu.VMEM((2, 128, 128), f32),
            pltpu.VMEM((PLANE, 3, 8, 128), f32),
            pltpu.VMEM((PLANE, 3, 8, 128), f32),
            pltpu.VMEM((8, 2, 8, 128), f32),
            pltpu.VMEM((GROUP, 8, 2, 8, 128), f32),
            pltpu.VMEM((PLANE, 2, 8, 128), f32),
            pltpu.VMEM((PLANE, 2, 8, 128), f32),
            pltpu.SemaphoreType.REGULAR,
            dma, dma((2,)), dma((2,)), dma((2, 4)), dma((2, 4)),
            dma((PLANE,)), dma((PLANE,)), dma((GROUP,)), dma((GROUP,)), dma((PLANE,)), dma((PLANE,)),
        ],
        compiler_params=pltpu.CompilerParams(
            collective_id=1, has_side_effects=True, vmem_limit_bytes=40 * 1024 * 1024),
        name="front",
    )(widths, region, sky)


WIDE = 4


def weights_of(grams, priors, cheb_t, keep):
    lanes = lax.broadcasted_iota(jnp.int32, (8, 128), 1)
    subs = lax.broadcasted_iota(jnp.int32, (8, 128), 0)
    mats = []
    for band in range(2):
        blocks = []
        for i in range(16):
            block = grams[band][i * 8:i * 8 + 8, :]
            diag = jnp.where(lanes == subs + 8 * i, priors[band], 0.0)
            blocks.append(block / 524288.0 + diag)
        blocks.append(cheb_t)
        mats.append(blocks)
    for k in range(0, 128, WIDE):
        at, off = k // 8, k % 8
        for band in range(2):
            m = mats[band]
            cols = [[jnp.broadcast_to(b[:, k + p:k + p + 1], (8, 128)) for b in m] for p in range(WIDE)]
            hit = (lanes >= k) & (lanes < k + WIDE)
            rows = [jnp.where(hit[0:1], jnp.where(lanes[0:1] == k + i, -1.0, 0.0), m[at][off + i:off + i + 1, :])
                    for i in range(WIDE)]
            d = [[cols[p][at][off + i:off + i + 1, :] for p in range(WIDE)] for i in range(WIDE)]
            inv = []
            for i in range(WIDE):
                inv.append(1.0 / d[i][i])
                for l in range(i + 1, WIDE):
                    t = d[l][i] * inv[i]
                    rows[l] = rows[l] - t * rows[i]
                    for j in range(i + 1, WIDE):
                        d[l][j] = d[l][j] - t * d[i][j]
            for i in reversed(range(WIDE)):
                line = rows[i]
                for j in range(i + 1, WIDE):
                    line = line - d[i][j] * rows[j]
                rows[i] = line * inv[i]
            fresh = []
            for index, b in enumerate(m):
                b = jnp.where(hit, 0.0, b)
                for p in range(WIDE):
                    b = b - cols[p][index] * rows[p]
                fresh.append(b)
            mats[band] = fresh
    out = []
    for band in range(2):
        mixed = mats[band][16] * keep
        kept = cheb_t * keep
        small = lax.dot_general(kept, mixed, (((1,), (1,)), ((), ())), precision=HIGH,
                                preferred_element_type=jnp.float32)
        eye = (lax.broadcasted_iota(jnp.int32, (8, 8), 0) == lax.broadcasted_iota(jnp.int32, (8, 8), 1))
        small = small + jnp.where(eye, 1.0 - keep[:, 0:8], 0.0)
        out.append((small, mixed))
    weights = []
    for small, mixed in out:
        for k in range(8):
            fac = small[:, k:k + 1]
            inv = 1.0 / fac[k:k + 1, :]
            shift = jnp.where(subs[:, 0:1] == k, 1.0, 0.0)
            fac = fac - shift
            srow = small[k:k + 1, :] * inv
            mrow = mixed[k:k + 1, :] * inv
            small = small - fac * srow
            mixed = mixed - fac * mrow
        weights.append(mixed)
    return weights


def chebyshev_rows():
    lane = lax.broadcasted_iota(jnp.int32, (8, 128), 1).astype(jnp.float32)
    order = lax.broadcasted_iota(jnp.int32, (8, 128), 0)
    position = (2.0 * lane + 1.0) / CHANS - 1.0
    terms = [jnp.ones_like(position), position]
    rows = jnp.where(order == 0, terms[0], position)
    for m in range(2, MMAX):
        terms.append(2.0 * position * terms[-1] - terms[-2])
        rows = jnp.where(order == m, terms[-1], rows)
    return rows


def back_kernel(region_ref, rank_ref, gram_ref, prior_ref, bands_ref, out_ref, proj, flat, ready, sems):
    cheb_t = chebyshev_rows()
    rank = rank_ref[region_ref[0, 0]]
    keep = jnp.where(lax.broadcasted_iota(jnp.int32, (8, 128), 0) < rank, 1.0, 0.0)
    weights = weights_of([gram_ref[0], gram_ref[1]], [prior_ref[0:1, :], prior_ref[1:2, :]], cheb_t, keep)
    kept = cheb_t * keep
    for band in range(2):
        part = lax.dot_general(kept, weights[band], (((0,), (0,)), ((), ())), precision=HIGH,
                               preferred_element_type=jnp.float32)
        proj[:, 128 * band:128 * band + 128] = part.astype(jnp.bfloat16)

    def put(slot, base):
        return pltpu.make_async_copy(ready.at[slot], out_ref.at[:, pl.ds(base, 16), :], sems.at[slot])

    def block(step, carry):
        for slot in range(2):
            base = pl.multiple_of(step * 32 + slot * 16, 16)
            for y in range(0, 16, 2):
                pair = jnp.concatenate([bands_ref[base + y], bands_ref[base + y + 1]], axis=1)
                removed = jnp.dot(proj[...], pair, preferred_element_type=jnp.float32)
                wide = pair.astype(jnp.float32)
                result = wide[0:128] + wide[128:256] - removed
                flat[pl.ds(2048 * slot + y, 128, stride=16), :] = result[:, 0:128]
                flat[pl.ds(2048 * slot + y + 1, 128, stride=16), :] = result[:, 128:256]

            @pl.when(step > 0)
            def _(slot=slot):
                put(slot, 0).wait()

            ready[slot] = flat[2048 * slot:2048 * slot + 2048, :].reshape(128, 16, 128).astype(jnp.bfloat16)
            put(slot, base).start()
        return carry

    lax.fori_loop(0, 8, block, 0)
    put(0, 0).wait()
    put(1, 0).wait()


def back(region, ranks, grams, prior_var, bands):
    whole = pl.BlockSpec(memory_space=pltpu.VMEM)
    bands = pltpu.with_memory_space_constraint(bands, pltpu.VMEM)
    return pl.pallas_call(
        back_kernel,
        out_shape=jax.ShapeDtypeStruct((128, 256, 128), jnp.bfloat16),
        in_specs=[pl.BlockSpec(memory_space=pltpu.SMEM)] * 2 + [whole] * 3,
        out_specs=pl.BlockSpec(memory_space=pl.ANY),
        scratch_shapes=[pltpu.VMEM((128, 256), jnp.bfloat16), pltpu.VMEM((4096, 128), jnp.float32),
                        pltpu.VMEM((2, 128, 16, 128), jnp.bfloat16), pltpu.SemaphoreType.DMA((2,))],
        compiler_params=pltpu.CompilerParams(vmem_limit_bytes=16 * 1024 * 1024),
        name="back",
    )(region, ranks, grams, prior_var, bands)


def local(sky, kernel_widths, prior_var, tile_region, region_rank):
    bands, own_gram = front(kernel_widths, tile_region, sky)
    return back(tile_region, region_rank, own_gram, prior_var, bands)


def solution(mesh):
    return jax.shard_map(
        local,
        mesh=mesh,
        in_specs=(P(None, "row", "col"), P(), P(), P("row", "col"), P()),
        out_specs=P(None, "row", "col"),
        check_vma=False,
    )
```
